32 devices in a mesh: dp: 4 (over y, core), expert: 8 (over z, x).
Axes of the slice: x: 2, y: 2, z: 4, core: 2. Of those that a mesh axis runs over, the one named last changes fastest.
Arguments:
- patches: bfloat16 [16384, 768], P(('dp', 'expert')), may hold values from -6 to 6
- owner_slot: int32 [128], P(('dp', 'expert')), may hold values from 0 to 127, as said below
- segment_ids: int32 [16384], P(('dp', 'expert')), may hold values from 0 to 127, as said below
- block_mask: int32 [128, 4], P(('dp', 'expert')), may hold values from 0 to 1, as said below
- project_in: bfloat16 [768, 2304], replicated, may hold values from -30 to 30
- project_out: bfloat16 [768, 768], replicated, may hold values from -0.21875 to 0.21875
- slot_keys: bfloat16 [768, 32], replicated, may hold values from -30 to 30
- expert_in: bfloat16 [32, 768, 3072], P(('dp', 'expert')), may hold values from -0.21875 to 0.21875
- expert_out: bfloat16 [32, 3072, 768], P(('dp', 'expert')), may hold values from -0.109375 to 0.109375
Outputs:
- layer_out: bfloat16 [16384, 768], P(('dp', 'expert'))
The draws below stay inside these ranges and needn't reach their ends.
Inputs may be any that keep to these rules, and one draw needn't show every extreme that they name: A permutation of the 128 blocks. Devices are numbered over dp then expert, and block g is read by device g // 4; it goes to device owner_slot[g] // 4, which has the same index along expert. Each reading device sends exactly 1 block to each of 4 distinct devices along dp, and each device receives exactly 4 blocks. `segment_ids`: Non-decreasing; the rows of run o (rows o * 512 to o * 512 + 511) carry the image numbers o * 4 to o * 4 + 3, each on one row or more. block_mask[o * 4 + a, b] is 1 when blocks a and b of run o hold rows of a common image, else 0.
All inputs are finite; a program needn't handle non-finite values.
Results may differ from the reference program's by a relative error of at most 0.0095.
The reference program's roundings to bfloat16 on the way count: a program that leaves them out, or rounds other values in their place, can miss the bound.
Values may be sent and summed in bfloat16 or wider, within the bound.
No kernel may reach another device: no remote copies, remote signals or barrier semaphores. Data moves between devices by JAX's collectives and lax.ppermute only.
A program may use at most 128 MiB of HBM per device.

```python
import jax
import jax.numpy as jnp
from jax import lax

D = 768
HID = 3072
HEADS = 12
HEAD = 64
BLOCK = 128
BLK_DEV = 4
EXPERTS = 32
TOK_DEV = 512
IMG_DEV = 4
IMAGES = 128
NBLK = 128
TOKENS = 16384
N_DP = 4
N_EXPERT = 8
DEVICES = 32


def permute_each(key, count, length):
    subkeys = jax.random.split(key, count)

    def permute_one(subkey):
        return jax.random.permutation(subkey, length).astype(jnp.int32)
    return jax.vmap(permute_one)(subkeys)


def draw_owner_slot(key, part):
    group = min(N_DP, BLK_DEV)
    shifts = permute_each(jax.random.fold_in(key, 11), N_EXPERT, N_DP)
    orders = permute_each(jax.random.fold_in(key, 12), DEVICES, BLK_DEV)
    reader = jnp.arange(DEVICES, dtype=jnp.int32)
    reader_data = reader // N_EXPERT
    reader_column = reader % N_EXPERT
    chosen = jnp.take_along_axis(shifts[reader_column], orders % group, axis=1)
    owner_data = (reader_data[:, None] + chosen) % N_DP
    owner_device = owner_data * N_EXPERT + reader_column[:, None]
    return (owner_device * BLK_DEV + orders).reshape(-1).astype(jnp.int32)


def image_layout(key):
    tok_dev = BLK_DEV * BLOCK
    subkeys = jax.random.split(jax.random.fold_in(key, 21), DEVICES)

    def one_owner(subkey):
        cuts = jax.random.permutation(subkey, tok_dev - 1)[:BLK_DEV - 1].astype(jnp.int32) + 1
        cuts = jnp.sort(cuts)
        position = jnp.arange(tok_dev, dtype=jnp.int32)
        return jnp.sum((position[:, None] >= cuts[None, :]).astype(jnp.int32), axis=1)
    return jax.vmap(one_owner)(subkeys)


def draw_segment_ids(key, part):
    local = image_layout(key)
    owner = jnp.arange(DEVICES, dtype=jnp.int32)[:, None]
    return (local + owner * BLK_DEV).reshape(-1).astype(jnp.int32)


def draw_block_mask(key, part):
    local = image_layout(key).reshape(DEVICES, BLK_DEV, BLOCK)
    first = local[:, :, 0]
    last = local[:, :, BLOCK - 1]
    lower = jnp.maximum(first[:, :, None], first[:, None, :])
    upper = jnp.minimum(last[:, :, None], last[:, None, :])
    return (lower <= upper).astype(jnp.int32).reshape(DEVICES * BLK_DEV, BLK_DEV)


def draw_project_in(key, part):
    base = jax.random.normal(jax.random.fold_in(key, 31), (D, 3 * D), jnp.float32) * D ** (-0.5)
    return jnp.clip(base, -30.0, 30.0).astype(jnp.bfloat16)


def draw_slot_keys(key, part):
    base = jax.random.normal(jax.random.fold_in(key, 41), (D, EXPERTS), jnp.float32) * D ** (-0.5)
    return jnp.clip(base, -30.0, 30.0).astype(jnp.bfloat16)


def block_levels(own_key, shape, cuts, low, top_value):
    factor_of, own = 1.0, jax.random.fold_in(own_key, 6)
    for dim, blocks in cuts:
        steps = jnp.exp(jax.random.uniform(jax.random.fold_in(own, dim), (blocks,), jnp.float32, low / len(cuts), top_value / len(cuts)))
        factor_of = factor_of * jnp.repeat(steps, shape[dim] // blocks).reshape([-1 if axis == dim else 1 for axis in range(len(shape))])
    return factor_of


def scatter_about(rng, shape, spread, most, pieces=(), kind=jnp.bfloat16):
    array = spread * jax.random.normal(rng, shape, jnp.float32)
    if pieces:
        array = array * block_levels(rng, shape, pieces, -0.22, 0.18)
    return jnp.clip(array, -most, most).astype(kind)


def setup_inputs(seed: int = 0) -> dict:
    arg_keys = jax.random.split(jax.random.key(seed), 10)
    return {
        "patches": scatter_about(arg_keys[0], (TOKENS, D), 1.0, 6.0, ((0, 32),)),
        "owner_slot": draw_owner_slot(jax.random.fold_in(arg_keys[9], 71), 0),
        "segment_ids": draw_segment_ids(jax.random.fold_in(arg_keys[9], 71), 0),
        "block_mask": draw_block_mask(jax.random.fold_in(arg_keys[9], 71), 0),
        "project_in": draw_project_in(jax.random.fold_in(arg_keys[9], 71), 0),
        "project_out": scatter_about(arg_keys[5], (D, D), D ** -0.5, 0.21875),
        "slot_keys": draw_slot_keys(jax.random.fold_in(arg_keys[9], 71), 0),
        "expert_in": scatter_about(arg_keys[7], (EXPERTS, D, HID), D ** -0.5, 0.21875, ((0, 32),)),
        "expert_out": scatter_about(arg_keys[8], (EXPERTS, HID, D), HID ** -0.5, 0.109375, ((0, 32),)),
    }


EPS = 1e-06
NEGATIVE = -1e+30

def layer_norm(values):
    values = values.astype(jnp.float32)
    centred = values - lax.optimization_barrier(jnp.mean(values, axis=-1, keepdims=True))
    variance = lax.optimization_barrier(jnp.mean(centred * centred, axis=-1, keepdims=True))
    return centred * lax.rsqrt(variance + EPS)

def rounded(values):
    return lax.optimization_barrier(values.astype(jnp.bfloat16)).astype(jnp.float32)

def reference(patches, owner_slot, segment_ids, block_mask, project_in, project_out, slot_keys, expert_in, expert_out):
    width = patches.shape[1]
    highest = lax.Precision.HIGHEST
    blocks = patches.reshape(NBLK, BLOCK, width)
    ordered_blocks = jnp.zeros_like(blocks).at[owner_slot].set(blocks)
    ordered_all = ordered_blocks.reshape(DEVICES, TOK_DEV, width)
    seg_all = segment_ids.reshape(DEVICES, TOK_DEV)
    mask_all = block_mask.reshape(DEVICES, BLK_DEV, BLK_DEV)
    block_of = jnp.arange(TOK_DEV, dtype=jnp.int32) // BLOCK
    image_range = jnp.arange(IMG_DEV, dtype=jnp.int32)

    def front(inputs):
        ordered, seg_row, mask_row = inputs
        normed = layer_norm(ordered).astype(jnp.bfloat16)
        joint = rounded(jnp.dot(normed, project_in, preferred_element_type=jnp.float32))
        queries = joint[:, :width].reshape(TOK_DEV, HEADS, HEAD)
        key_rows = joint[:, width:2 * width].reshape(TOK_DEV, HEADS, HEAD)
        value_rows = joint[:, 2 * width:].reshape(TOK_DEV, HEADS, HEAD)
        linked = (seg_row[:, None] == seg_row[None, :]) & (mask_row[block_of][:, block_of] == 1)
        scores = jnp.einsum('qhd,khd->hqk', queries, key_rows, precision=highest) * HEAD ** (-0.5)
        scores = jnp.where(linked[None], scores, NEGATIVE)
        raised = jnp.exp(scores - lax.optimization_barrier(jnp.max(scores, axis=2, keepdims=True)))
        weights = rounded(raised / lax.optimization_barrier(jnp.sum(raised, axis=2, keepdims=True)))
        context = jnp.einsum('hqk,khd->qhd', weights, value_rows, precision=highest).reshape(TOK_DEV, width).astype(jnp.bfloat16)
        hidden = (ordered.astype(jnp.float32) + jnp.dot(context, project_out, preferred_element_type=jnp.float32)).astype(jnp.bfloat16)
        moe_normed = lax.optimization_barrier(layer_norm(hidden).astype(jnp.bfloat16))
        logits = jnp.dot(moe_normed, slot_keys, preferred_element_type=jnp.float32)
        local_image = seg_row % IMG_DEV
        member = local_image[None, :] == image_range[:, None]
        member_float = member.astype(jnp.float32)
        column_max = lax.optimization_barrier(jnp.max(jnp.where(member[:, :, None], logits[None], NEGATIVE), axis=1))
        raised_slots = jnp.exp(logits - column_max[local_image])
        totals = jnp.dot(member_float, raised_slots, precision=highest)
        dispatch = rounded(raised_slots / totals[local_image])
        slot_in = jnp.einsum('st,te,td->sed', member_float, dispatch, moe_normed.astype(jnp.float32), precision=highest).astype(jnp.bfloat16)
        slot_raised = jnp.exp(logits - lax.optimization_barrier(jnp.max(logits, axis=1, keepdims=True)))
        combine = (slot_raised / lax.optimization_barrier(jnp.sum(slot_raised, axis=1, keepdims=True))).astype(jnp.bfloat16)
        return (hidden, slot_in, combine, local_image)
    hidden_all, slot_all, combine_all, local_all = lax.map(front, (ordered_all, seg_all, mask_all))
    slots = jnp.swapaxes(slot_all.reshape(IMAGES, EXPERTS, width), 0, 1)

    def expert_step(inputs):
        slot_column, weight_in, weight_out = inputs
        inner = jnp.dot(slot_column, weight_in, preferred_element_type=jnp.float32)
        inner = jax.nn.gelu(inner, approximate=False).astype(jnp.bfloat16)
        return jnp.dot(inner, weight_out, preferred_element_type=jnp.float32).astype(jnp.bfloat16)
    produced = lax.map(expert_step, (slots, expert_in, expert_out))
    slot_out_all = jnp.swapaxes(produced, 0, 1).reshape(DEVICES, IMG_DEV, EXPERTS, width)

    def back(inputs):
        hidden, combine, local_image, slot_out = inputs
        member_float = (local_image[None, :] == image_range[:, None]).astype(jnp.float32)
        combine_float = lax.optimization_barrier(combine).astype(jnp.float32)
        mixture = jnp.einsum('st,te,sed->td', member_float, combine_float, slot_out.astype(jnp.float32), precision=highest)
        hidden_float = lax.optimization_barrier(hidden).astype(jnp.float32)
        return (hidden_float + mixture).astype(jnp.bfloat16)
    result = lax.map(back, (hidden_all, combine_all, local_all, slot_out_all))
    return result.reshape(TOKENS, width)
```

```python
import functools
import math

import jax
import jax.numpy as jnp
from jax import lax
from jax.experimental import pallas as pl
from jax.experimental.pallas import tpu as pltpu
from jax.sharding import PartitionSpec as P

HEAD = 64
LANES = 128
TAG_ROWS = 8
EPS = 1e-06
NEGATIVE = -1e30
AXES = ("dp", "expert")


def layer_norm(values):
    centred = values - jnp.mean(values, axis=-1, keepdims=True)
    variance = jnp.mean(centred * centred, axis=-1, keepdims=True)
    return centred * lax.rsqrt(variance + EPS)


def dot(a, b, dims=((1,), (0,))):
    return lax.dot_general(a, b, (dims, ((), ())), preferred_element_type=jnp.float32)


def front_kernel(
    self_ref,
    patches_ref,
    *refs,
    slots,
):
    arrived = refs[:slots]
    (
        query_mark_ref,
        key_mark_ref,
        member_ref,
        project_in_ref,
        project_out_ref,
        slot_keys_ref,
        hidden_ref,
        slot_in_ref,
        combine_ref,
        ordered_ref,
        joint_ref,
        context_ref,
    ) = refs[slots:]
    tok_count, width = ordered_ref.shape
    rows = arrived[0].shape[0] - TAG_ROWS

    def place_block(block, place):
        at = pl.ds(pl.multiple_of(place * rows, rows), rows)
        ordered_ref[at, :] = block
        normed = layer_norm(block.astype(jnp.float32)).astype(jnp.bfloat16)
        joint_ref[at, :] = dot(normed, project_in_ref[...]).astype(jnp.bfloat16)

    place_block(
        patches_ref[pl.ds(pl.multiple_of(self_ref[0] * rows, rows), rows), :], self_ref[1]
    )
    for ref in arrived:
        tag = jnp.max(ref[rows:, :LANES].astype(jnp.float32)).astype(jnp.int32)

        @pl.when(tag >= 0)
        def _():
            place_block(ref[:rows, :], tag)

    lane = lax.broadcasted_iota(jnp.int32, (1, LANES), 1)
    first = lane < HEAD
    ones = jnp.ones((tok_count, LANES), jnp.bfloat16)
    zero = jnp.zeros((), jnp.bfloat16)
    scale = HEAD ** (-0.5) * math.log2(math.e)
    for pair in range(width // LANES):
        at = pair * LANES
        query = joint_ref[:, at : at + LANES]
        key = joint_ref[:, width + at : width + at + LANES]
        value = joint_ref[:, 2 * width + at : 2 * width + at + LANES]
        keys = jnp.concatenate([key, key_mark_ref[...]], axis=1)
        values = jnp.concatenate([value, ones], axis=1)
        parts = []
        for keep in (first, ~first):
            queries = jnp.concatenate(
                [jnp.where(keep, query, zero), query_mark_ref[...]], axis=1
            )
            scores = dot(queries, keys, ((1,), (1,)))
            top = jnp.max(scores, axis=1, keepdims=True)
            raised = jnp.exp2((scores - top) * scale).astype(jnp.bfloat16)
            parts.append(dot(raised, values))
        picked = jnp.where(first, parts[0][:, :LANES], parts[1][:, :LANES])
        total = jnp.where(first, parts[0][:, LANES:], parts[1][:, LANES:])
        context_ref[:, at : at + LANES] = (picked / total).astype(jnp.bfloat16)

    hidden = (
        ordered_ref[...].astype(jnp.float32) + dot(context_ref[...], project_out_ref[...])
    ).astype(jnp.bfloat16)
    hidden_ref[...] = hidden
    moe_normed = layer_norm(hidden.astype(jnp.float32)).astype(jnp.bfloat16)
    logits = dot(moe_normed, slot_keys_ref[...])
    member = member_ref[...] > 0
    column_top = jnp.max(jnp.where(member, logits, NEGATIVE), axis=0, keepdims=True)
    column_raised = jnp.where(member, jnp.exp(logits - column_top), 0.0)
    dispatch = column_raised / jnp.sum(column_raised, axis=0, keepdims=True)
    slot_in = dot(dispatch.astype(jnp.bfloat16), moe_normed, ((0,), (0,)))
    slot_in_ref[...] = slot_in.astype(jnp.bfloat16).reshape(slot_in_ref.shape)
    row_top = jnp.max(logits, axis=1, keepdims=True)
    row_raised = jnp.where(member, jnp.exp(logits - row_top), 0.0)
    combine = row_raised / jnp.sum(row_raised, axis=1, keepdims=True)
    combine_ref[...] = combine.astype(jnp.bfloat16)


def expert_kernel(arrived_ref, expert_in_ref, expert_out_ref, produced_ref, total_ref):
    step = pl.program_id(0)
    rows = total_ref.shape[0]
    slots = arrived_ref[...].reshape(rows, total_ref.shape[1])
    inner = dot(slots, expert_in_ref[...])
    inner = 0.5 * inner * (1.0 + lax.erf(inner * math.sqrt(0.5)))
    part = dot(inner.astype(jnp.bfloat16), expert_out_ref[...])

    @pl.when(step == 0)
    def _():
        total_ref[...] = part

    @pl.when(step > 0)
    def _():
        total_ref[...] += part

    @pl.when(step == pl.num_programs(0) - 1)
    def _():
        produced_ref[...] = total_ref[...].astype(jnp.bfloat16).reshape(produced_ref.shape)


def combine_kernel(hidden_ref, combine_ref, returned_ref, out_ref):
    returned = returned_ref[...].reshape(combine_ref.shape[1], hidden_ref.shape[1])
    mixture = dot(combine_ref[...], returned)
    out_ref[...] = (hidden_ref[...].astype(jnp.float32) + mixture).astype(jnp.bfloat16)


def whole(memory_space=pltpu.VMEM):
    return pl.BlockSpec(memory_space=memory_space)


def per_device(
    patches,
    owner_slot,
    segment_ids,
    block_mask,
    project_in,
    project_out,
    slot_keys,
    expert_in,
    expert_out,
):
    tok_count, width = patches.shape
    blk_count = owner_slot.shape[0]
    rows = tok_count // blk_count
    data_count = lax.axis_size("dp")
    column_count = lax.axis_size("expert")
    expert_count = slot_keys.shape[1]
    hidden_width = expert_in.shape[2]
    me = lax.axis_index("dp")

    target_data = owner_slot // blk_count // column_count
    target_place = owner_slot % blk_count
    block_index = jnp.arange(blk_count, dtype=jnp.int32)

    def route(flip):
        chosen = target_data == me ^ flip
        source = jnp.sum(jnp.where(chosen, block_index, 0))
        place = jnp.sum(jnp.where(chosen, target_place + 1, 0)) - 1
        return source, place

    arrived = []
    for flip in [*range(2, data_count), 1]:
        source, place = route(flip)
        block = lax.dynamic_slice(patches, (source * rows, 0), (rows, width))
        tag = jnp.full((TAG_ROWS, width), place.astype(jnp.bfloat16))
        arrived.append(
            lax.ppermute(
                jnp.concatenate([block, tag], axis=0),
                "dp",
                [(i, i ^ flip) for i in range(data_count)],
            )
        )
    self_info = jnp.stack(route(0))

    local_image = segment_ids % blk_count
    block_of = jnp.arange(tok_count, dtype=jnp.int32) // rows
    column = jnp.arange(LANES, dtype=jnp.int32)[None, :]
    image_is = local_image[:, None] == column
    block_is = block_of[:, None] == column - blk_count
    unlinked = jnp.repeat(block_mask != 1, rows, axis=0)
    blocked = jnp.pad(unlinked, ((0, 0), (blk_count, LANES - 2 * blk_count)))
    query_mark = jnp.where(image_is | blocked, NEGATIVE, 0.0).astype(jnp.bfloat16)
    key_mark = (jnp.where(column < blk_count, ~image_is, block_is)).astype(jnp.bfloat16)
    columns = expert_count * blk_count
    column_image = jnp.arange(columns, dtype=jnp.int32)[None, :] % blk_count
    member = (local_image[:, None] == column_image).astype(jnp.float32)
    slot_keys_wide = jnp.repeat(slot_keys, blk_count, axis=1)

    hidden, slot_in, combine = pl.pallas_call(
        functools.partial(front_kernel, slots=len(arrived)),
        out_shape=(
            jax.ShapeDtypeStruct((tok_count, width), jnp.bfloat16),
            jax.ShapeDtypeStruct((expert_count, blk_count, width), jnp.bfloat16),
            jax.ShapeDtypeStruct((tok_count, columns), jnp.bfloat16),
        ),
        in_specs=[whole(pltpu.SMEM)] + [whole()] * (7 + len(arrived)),
        out_specs=(whole(),) * 3,
        scratch_shapes=[
            pltpu.VMEM((tok_count, width), jnp.bfloat16),
            pltpu.VMEM((tok_count, 3 * width), jnp.bfloat16),
            pltpu.VMEM((tok_count, width), jnp.bfloat16),
        ],
        name="front",
    )(
        self_info,
        patches,
        *arrived,
        query_mark,
        key_mark,
        member,
        project_in,
        project_out,
        slot_keys_wide,
    )
    slots_here = lax.all_to_all(slot_in, AXES, split_axis=0, concat_axis=0, tiled=True)
    step = min(hidden_width, 768)
    row_count = expert_count * blk_count
    produced = pl.pallas_call(
        expert_kernel,
        out_shape=jax.ShapeDtypeStruct(slots_here.shape, jnp.bfloat16),
        grid=(hidden_width // step,),
        in_specs=[
            pl.BlockSpec(slots_here.shape, lambda i: (0, 0, 0)),
            pl.BlockSpec((None, width, step), lambda i: (0, 0, i)),
            pl.BlockSpec((None, step, width), lambda i: (0, i, 0)),
        ],
        out_specs=pl.BlockSpec(slots_here.shape, lambda i: (0, 0, 0)),
        scratch_shapes=[pltpu.VMEM((row_count, width), jnp.float32)],
        name="expert",
    )(slots_here, expert_in, expert_out)
    returned = lax.all_to_all(produced, AXES, split_axis=0, concat_axis=0, tiled=True)
    return pl.pallas_call(
        combine_kernel,
        out_shape=jax.ShapeDtypeStruct((tok_count, width), jnp.bfloat16),
        in_specs=[whole()] * 3,
        out_specs=whole(),
        name="combine",
    )(hidden, combine, returned)


def solution(mesh):
    in_specs = (
        P(AXES, None),
        P(AXES),
        P(AXES),
        P(AXES, None),
        P(),
        P(),
        P(),
        P(AXES, None, None),
        P(AXES, None, None),
    )
    return jax.shard_map(
        per_device, mesh=mesh, in_specs=in_specs, out_specs=P(AXES, None), check_vma=False
    )
```

```python
import functools
import math

import jax
import jax.numpy as jnp
from jax import lax
from jax.experimental import pallas as pl
from jax.experimental.pallas import tpu as pltpu
from jax.sharding import PartitionSpec as P

HEAD = 64
LANES = 128
TAG_ROWS = 8
EPS = 1e-06
NEGATIVE = -1e30
AXES = ("dp", "expert")
VMEM_LIMIT = 24 << 20


def layer_norm(values):
    centred = values - jnp.mean(values, axis=-1, keepdims=True)
    variance = jnp.mean(centred * centred, axis=-1, keepdims=True)
    return centred * lax.rsqrt(variance + EPS)


def dot(a, b, dims=((1,), (0,))):
    return lax.dot_general(a, b, (dims, ((), ())), preferred_element_type=jnp.float32)


def route_of(owner_ref, target, columns):
    blk_count = owner_ref.shape[0]
    source = jnp.int32(0)
    place = jnp.int32(-1)
    for block in range(blk_count):
        owner = owner_ref[block]
        hit = owner // (blk_count * columns) == target
        source = jnp.where(hit, block, source)
        place = jnp.where(hit, owner % blk_count, place)
    return source, place


def send_kernel(owner_ref, patches_ref, *refs, flips, columns):
    sends, sems = refs[:-1], refs[-1]
    rows = sends[0].shape[0] - TAG_ROWS
    me = lax.axis_index("dp")
    copies = []
    for n, (flip, send) in enumerate(zip(flips, sends)):
        source, place = route_of(owner_ref, me ^ flip, columns)
        at = pl.ds(pl.multiple_of(source * rows, rows), rows)
        copy = pltpu.make_async_copy(patches_ref.at[at, :], send.at[:rows, :], sems.at[n])
        copy.start()
        send[rows:, :] = jnp.full((TAG_ROWS, send.shape[1]), place.astype(jnp.float32)).astype(
            jnp.bfloat16
        )
        copies.append(copy)
    for copy in copies:
        copy.wait()


def place_block(block, place, project_in, ordered_ref, joint_ref):
    rows = block.shape[0]
    at = pl.ds(pl.multiple_of(place * rows, rows), rows)
    ordered_ref[at, :] = block
    normed = layer_norm(block.astype(jnp.float32)).astype(jnp.bfloat16)
    joint_ref[at, :] = dot(normed, project_in).astype(jnp.bfloat16)


def place_arrived(ref, project_in_ref, ordered_ref, joint_ref):
    rows = ref.shape[0] - TAG_ROWS
    place = jnp.max(ref[rows:, :LANES].astype(jnp.float32)).astype(jnp.int32)

    @pl.when(place >= 0)
    def _():
        place_block(ref[:rows, :], place, project_in_ref[...], ordered_ref, joint_ref)


def prepare_kernel(
    owner_ref,
    block_mask_ref,
    segment_ref,
    slot_keys_ref,
    patches_ref,
    near_ref,
    *refs,
    columns,
):
    count = (len(refs) - 8) // 2
    sources, weights = refs[:count], refs[count : 2 * count]
    query_mark_ref, key_mark_ref, image_ref, slot_keys_wide_ref = refs[2 * count : 2 * count + 4]
    ordered_ref, joint_ref, own_ref, sems = refs[2 * count + 4 :]
    blk_count = owner_ref.shape[0]
    tok_count = ordered_ref.shape[0]
    rows = tok_count // blk_count
    copies = [
        pltpu.make_async_copy(source, weight, sems.at[n])
        for n, (source, weight) in enumerate(zip(sources, weights))
    ]
    source, place = route_of(owner_ref, lax.axis_index("dp"), columns)
    own_at = pl.ds(pl.multiple_of(source * rows, rows), rows)
    own_copy = pltpu.make_async_copy(patches_ref.at[own_at, :], own_ref, sems.at[count])
    own_copy.start()
    for copy in copies:
        copy.start()

    lane = lax.broadcasted_iota(jnp.int32, (1, LANES), 1)
    lane_float = lane.astype(jnp.float32)
    image = (segment_ref[...] % blk_count).astype(jnp.float32)
    image = jnp.transpose(jnp.broadcast_to(image, (LANES, tok_count)))
    image_ref[...] = image
    image_is = image == lane_float
    for block in range(blk_count):
        at = slice(block * rows, (block + 1) * rows)
        blocked = jnp.zeros((1, LANES), jnp.float32)
        for other in range(blk_count):
            value = jnp.where(block_mask_ref[block, other] == 1, 0.0, NEGATIVE)
            blocked = jnp.where(lane == blk_count + other, value, blocked)
        query_mark_ref[at, :] = jnp.where(image_is[at], NEGATIVE, blocked).astype(jnp.bfloat16)
        block_is = jnp.where(lane == blk_count + block, 1.0, 0.0)
        key_mark_ref[at, :] = jnp.where(
            lane < blk_count, jnp.where(image_is[at], 0.0, 1.0), block_is
        ).astype(jnp.bfloat16)
    experts, wide = slot_keys_ref.shape[1], slot_keys_wide_ref.shape[1]
    expert = lax.broadcasted_iota(jnp.int32, (experts, wide), 0)
    column = lax.broadcasted_iota(jnp.int32, (experts, wide), 1)
    spread = jnp.where(column // blk_count == expert, 1.0, 0.0).astype(jnp.bfloat16)
    slot_keys_wide_ref[...] = dot(slot_keys_ref[...], spread).astype(jnp.bfloat16)

    own_copy.wait()
    copies[0].wait()
    project_in_ref = weights[0]
    place_block(own_ref[...], place, project_in_ref[...], ordered_ref, joint_ref)
    place_arrived(near_ref, project_in_ref, ordered_ref, joint_ref)
    for copy in copies[1:]:
        copy.wait()


def front_kernel(*refs, slots):
    arrived = refs[:slots]
    (
        _,
        _,
        query_mark_ref,
        key_mark_ref,
        image_ref,
        project_in_ref,
        project_out_ref,
        slot_keys_ref,
        ordered_ref,
        joint_ref,
        hidden_ref,
        slot_in_ref,
        combine_ref,
        context_ref,
    ) = refs[slots:]
    tok_count, width = ordered_ref.shape
    for ref in arrived:
        place_arrived(ref, project_in_ref, ordered_ref, joint_ref)

    lane = lax.broadcasted_iota(jnp.int32, (1, LANES), 1)
    first = lane < HEAD
    ones = jnp.ones((tok_count, LANES), jnp.bfloat16)
    zero = jnp.zeros((), jnp.bfloat16)
    scale = HEAD ** (-0.5) * math.log2(math.e)
    for pair in range(width // LANES):
        at = pair * LANES
        query = joint_ref[:, at : at + LANES]
        key = joint_ref[:, width + at : width + at + LANES]
        value = joint_ref[:, 2 * width + at : 2 * width + at + LANES]
        keys = jnp.concatenate([key, key_mark_ref[...]], axis=1)
        values = jnp.concatenate([value, ones], axis=1)
        parts = []
        for keep in (first, ~first):
            queries = jnp.concatenate(
                [jnp.where(keep, query, zero), query_mark_ref[...]], axis=1
            )
            scores = dot(queries, keys, ((1,), (1,)))
            top = jnp.max(scores, axis=1, keepdims=True)
            raised = jnp.exp2((scores - top) * scale).astype(jnp.bfloat16)
            parts.append(dot(raised, values))
        picked = jnp.where(first, parts[0][:, :LANES], parts[1][:, :LANES])
        total = jnp.where(first, parts[0][:, LANES:], parts[1][:, LANES:])
        context_ref[:, at : at + LANES] = (picked / total).astype(jnp.bfloat16)

    hidden = (
        ordered_ref[...].astype(jnp.float32) + dot(context_ref[...], project_out_ref[...])
    ).astype(jnp.bfloat16)
    hidden_ref[...] = hidden
    moe_normed = layer_norm(hidden.astype(jnp.float32)).astype(jnp.bfloat16)
    logits = dot(moe_normed, slot_keys_ref[...])
    blk_count = slot_in_ref.shape[1]
    image_here = image_ref[...] == (lane % blk_count).astype(jnp.float32)
    member = jnp.concatenate([image_here] * (logits.shape[1] // LANES), axis=1)
    column_top = jnp.max(jnp.where(member, logits, NEGATIVE), axis=0, keepdims=True)
    column_raised = jnp.where(member, jnp.exp(logits - column_top), 0.0)
    dispatch = column_raised / jnp.sum(column_raised, axis=0, keepdims=True)
    slot_in = dot(dispatch.astype(jnp.bfloat16), moe_normed, ((0,), (0,)))
    slot_in_ref[...] = slot_in.astype(jnp.bfloat16).reshape(slot_in_ref.shape)
    row_top = jnp.max(logits, axis=1, keepdims=True)
    row_raised = jnp.where(member, jnp.exp(logits - row_top), 0.0)
    combine = row_raised / jnp.sum(row_raised, axis=1, keepdims=True)
    combine_ref[...] = combine.astype(jnp.bfloat16)


def expert_kernel(arrived_ref, expert_in_ref, expert_out_ref, produced_ref, total_ref):
    rows, width = total_ref.shape
    slots = arrived_ref[...].reshape(rows, width)
    hidden_width = expert_in_ref.shape[2]
    step = math.gcd(hidden_width, 768)
    for at in range(0, hidden_width, step):
        inner = dot(slots, expert_in_ref[0, :, at : at + step])
        inner = 0.5 * inner * (1.0 + lax.erf(inner * math.sqrt(0.5)))
        part = dot(inner.astype(jnp.bfloat16), expert_out_ref[0, at : at + step, :])
        total_ref[...] = part if at == 0 else total_ref[...] + part
    produced_ref[...] = total_ref[...].astype(jnp.bfloat16).reshape(produced_ref.shape)


def combine_kernel(hidden_ref, combine_ref, returned_ref, out_ref):
    returned = returned_ref[...].reshape(combine_ref.shape[1], hidden_ref.shape[1])
    mixture = dot(combine_ref[...], returned)
    out_ref[...] = (hidden_ref[...].astype(jnp.float32) + mixture).astype(jnp.bfloat16)


def resident(*arrays, memory_space=pltpu.VMEM):
    return [pltpu.with_memory_space_constraint(array, memory_space) for array in arrays]


def whole(memory_space=pltpu.VMEM):
    return pl.BlockSpec(memory_space=memory_space)


def per_device(
    patches,
    owner_slot,
    segment_ids,
    block_mask,
    project_in,
    project_out,
    slot_keys,
    expert_in,
    expert_out,
):
    tok_count, width = patches.shape
    blk_count = owner_slot.shape[0]
    rows = tok_count // blk_count
    data_count = lax.axis_size("dp")
    column_count = lax.axis_size("expert")
    expert_count = slot_keys.shape[1]
    columns = expert_count * blk_count
    params = pltpu.CompilerParams(vmem_limit_bytes=VMEM_LIMIT)

    flips = [*range(2, data_count), 1]
    sends = pl.pallas_call(
        functools.partial(send_kernel, flips=flips, columns=column_count),
        out_shape=[pltpu.VMEM((rows + TAG_ROWS, width), jnp.bfloat16)] * len(flips),
        in_specs=[whole(pltpu.SMEM), whole(pltpu.HBM)],
        out_specs=[whole()] * len(flips),
        scratch_shapes=[pltpu.SemaphoreType.DMA((len(flips),))],
        compiler_params=params,
        name="send",
    )(*resident(owner_slot, patches, memory_space=pltpu.HBM))
    arrived = [
        lax.ppermute(send, "dp", [(i, i ^ flip) for i in range(data_count)])
        for flip, send in zip(flips, sends)
    ]
    far, near = arrived[:-1], arrived[-1]

    streamed = [project_in, project_out, expert_in, expert_out]
    prepared = pl.pallas_call(
        functools.partial(prepare_kernel, columns=column_count),
        out_shape=[pltpu.VMEM(w.shape, w.dtype) for w in streamed]
        + [
            pltpu.VMEM((tok_count, LANES), jnp.bfloat16),
            pltpu.VMEM((tok_count, LANES), jnp.bfloat16),
            pltpu.VMEM((tok_count, LANES), jnp.float32),
            pltpu.VMEM((width, columns), jnp.bfloat16),
            pltpu.VMEM((tok_count, width), jnp.bfloat16),
            pltpu.VMEM((tok_count, 3 * width), jnp.bfloat16),
        ],
        in_specs=[whole(pltpu.SMEM)] * 2
        + [whole()] * 2
        + [whole(pltpu.HBM), whole()]
        + [whole(pltpu.HBM)] * len(streamed),
        out_specs=[whole()] * (len(streamed) + 6),
        scratch_shapes=[
            pltpu.VMEM((rows, width), jnp.bfloat16),
            pltpu.SemaphoreType.DMA((len(streamed) + 1,)),
        ],
        compiler_params=params,
        name="prepare",
    )(
        *resident(owner_slot, block_mask, memory_space=pltpu.HBM),
        segment_ids.reshape(1, tok_count),
        slot_keys,
        *resident(patches, memory_space=pltpu.HBM),
        *resident(near),
        *resident(*streamed, memory_space=pltpu.HBM),
    )
    project_in, project_out, expert_in, expert_out = prepared[:4]
    query_mark, key_mark, image, slot_keys_wide, ordered, joint = prepared[4:]

    late = len(far)
    _, _, hidden, slot_in, combine = pl.pallas_call(
        functools.partial(front_kernel, slots=late),
        out_shape=(
            pltpu.VMEM((tok_count, width), jnp.bfloat16),
            pltpu.VMEM((tok_count, 3 * width), jnp.bfloat16),
            pltpu.VMEM((tok_count, width), jnp.bfloat16),
            pltpu.VMEM((expert_count, blk_count, width), jnp.bfloat16),
            pltpu.VMEM((tok_count, columns), jnp.bfloat16),
        ),
        in_specs=[whole()] * (8 + late),
        out_specs=(whole(),) * 5,
        input_output_aliases={late: 0, late + 1: 1},
        scratch_shapes=[pltpu.VMEM((tok_count, width), jnp.bfloat16)],
        compiler_params=params,
        name="front",
    )(
        *resident(
            *far,
            ordered,
            joint,
            query_mark,
            key_mark,
            image,
            project_in,
            project_out,
            slot_keys_wide,
        )
    )
    slots_here = lax.all_to_all(slot_in, AXES, split_axis=0, concat_axis=0, tiled=True)
    produced = pl.pallas_call(
        expert_kernel,
        out_shape=pltpu.VMEM(slots_here.shape, jnp.bfloat16),
        in_specs=[whole()] * 3,
        out_specs=whole(),
        scratch_shapes=[pltpu.VMEM((columns, width), jnp.float32)],
        compiler_params=params,
        name="expert",
    )(*resident(slots_here, expert_in, expert_out))
    returned = lax.all_to_all(produced, AXES, split_axis=0, concat_axis=0, tiled=True)
    return pl.pallas_call(
        combine_kernel,
        out_shape=jax.ShapeDtypeStruct((tok_count, width), jnp.bfloat16),
        in_specs=[whole()] * 3,
        out_specs=whole(),
        compiler_params=params,
        name="combine",
    )(*resident(hidden, combine, returned))


def solution(mesh):
    in_specs = (
        P(AXES, None),
        P(AXES),
        P(AXES),
        P(AXES, None),
        P(),
        P(),
        P(),
        P(AXES, None, None),
        P(AXES, None, None),
    )
    return jax.shard_map(
        per_device, mesh=mesh, in_specs=in_specs, out_specs=P(AXES, None), check_vma=False
    )
```

```python
import functools
import math

import jax
import jax.numpy as jnp
from jax import lax
from jax.experimental import pallas as pl
from jax.experimental.pallas import tpu as pltpu
from jax.sharding import PartitionSpec as P

HEAD = 64
LANES = 128
TAG_ROWS = 8
EPS = 1e-06
NEGATIVE = -1e30
AXES = ("dp", "expert")
VMEM_LIMIT = 24 << 20


def layer_norm(values):
    centred = values - jnp.mean(values, axis=-1, keepdims=True)
    variance = jnp.mean(centred * centred, axis=-1, keepdims=True)
    return centred * lax.rsqrt(variance + EPS)


def dot(a, b, dims=((1,), (0,))):
    return lax.dot_general(a, b, (dims, ((), ())), preferred_element_type=jnp.float32)


def route_of(owner_ref, target, columns):
    blk_count = owner_ref.shape[0]
    source = jnp.int32(0)
    place = jnp.int32(-1)
    for block in range(blk_count):
        owner = owner_ref[block]
        hit = owner // (blk_count * columns) == target
        source = jnp.where(hit, block, source)
        place = jnp.where(hit, owner % blk_count, place)
    return source, place


def send_kernel(owner_ref, patches_ref, *refs, flips, columns):
    sends, sems = refs[:-1], refs[-1]
    rows = sends[0].shape[0] - TAG_ROWS
    me = lax.axis_index("dp")
    copies = []
    for n, (flip, send) in enumerate(zip(flips, sends)):
        source, place = route_of(owner_ref, me ^ flip, columns)
        at = pl.ds(pl.multiple_of(source * rows, rows), rows)
        copy = pltpu.make_async_copy(patches_ref.at[at, :], send.at[:rows, :], sems.at[n])
        copy.start()
        send[rows:, :] = jnp.full((TAG_ROWS, send.shape[1]), place.astype(jnp.float32)).astype(
            jnp.bfloat16
        )
        copies.append(copy)
    for copy in copies:
        copy.wait()


def place_block(block, place, project_in_ref, ordered_ref, joint_ref):
    rows = block.shape[0]
    at = pl.ds(pl.multiple_of(place * rows, rows), rows)
    ordered_ref[at, :] = block
    normed = layer_norm(block.astype(jnp.float32)).astype(jnp.bfloat16)
    joint_ref[at, :] = dot(normed, project_in_ref[...]).astype(jnp.bfloat16)


def place_arrived(ref, project_in_ref, ordered_ref, joint_ref, certain):
    rows = ref.shape[0] - TAG_ROWS
    place = jnp.max(ref[rows:, :LANES].astype(jnp.float32)).astype(jnp.int32)

    def fill():
        place_block(ref[:rows, :], place, project_in_ref, ordered_ref, joint_ref)

    if certain:
        fill()
    else:
        pl.when(place >= 0)(fill)


def prepare_kernel(
    owner_ref,
    block_mask_ref,
    segment_ref,
    slot_keys_ref,
    patches_ref,
    near_ref,
    *refs,
    columns,
    certain,
):
    count = (len(refs) - 8) // 2
    sources, weights = refs[:count], refs[count : 2 * count]
    query_mark_ref, key_mark_ref, image_ref, slot_keys_wide_ref = refs[2 * count : 2 * count + 4]
    ordered_ref, joint_ref, own_ref, sems = refs[2 * count + 4 :]
    blk_count = owner_ref.shape[0]
    tok_count = ordered_ref.shape[0]
    rows = tok_count // blk_count
    copies = [
        pltpu.make_async_copy(source, weight, sems.at[n])
        for n, (source, weight) in enumerate(zip(sources, weights))
    ]
    source, place = route_of(owner_ref, lax.axis_index("dp"), columns)
    own_at = pl.ds(pl.multiple_of(source * rows, rows), rows)
    own_copy = pltpu.make_async_copy(patches_ref.at[own_at, :], own_ref, sems.at[count])
    own_copy.start()
    for copy in copies:
        copy.start()

    lane = lax.broadcasted_iota(jnp.int32, (1, LANES), 1)
    lane_float = lane.astype(jnp.float32)
    image = (segment_ref[...] % blk_count).astype(jnp.float32)
    image = jnp.transpose(jnp.broadcast_to(image, (LANES, tok_count)))
    image_ref[...] = image
    image_is = image == lane_float
    for block in range(blk_count):
        at = slice(block * rows, (block + 1) * rows)
        blocked = jnp.zeros((1, LANES), jnp.float32)
        for other in range(blk_count):
            value = jnp.where(block_mask_ref[block, other] == 1, 0.0, NEGATIVE)
            blocked = jnp.where(lane == blk_count + other, value, blocked)
        query_mark_ref[at, :] = jnp.where(image_is[at], NEGATIVE, blocked).astype(jnp.bfloat16)
        block_is = jnp.where(lane == blk_count + block, 1.0, 0.0)
        key_mark_ref[at, :] = jnp.where(
            lane < blk_count, jnp.where(image_is[at], 0.0, 1.0), block_is
        ).astype(jnp.bfloat16)
    wide, experts = slot_keys_wide_ref.shape[0], slot_keys_ref.shape[1]
    column = lax.broadcasted_iota(jnp.int32, (wide, experts), 0)
    expert = lax.broadcasted_iota(jnp.int32, (wide, experts), 1)
    spread = jnp.where(column // blk_count == expert, 1.0, 0.0).astype(jnp.bfloat16)
    slot_keys_wide_ref[...] = dot(spread, slot_keys_ref[...], ((1,), (1,))).astype(jnp.bfloat16)

    own_copy.wait()
    copies[0].wait()
    project_in_ref = weights[0]
    place_block(own_ref[...], place, project_in_ref, ordered_ref, joint_ref)
    place_arrived(near_ref, project_in_ref, ordered_ref, joint_ref, certain)
    for copy in copies[1:]:
        copy.wait()


def middle_kernel(*refs, certain):
    *arrived, project_in_ref, _, _, ordered_ref, joint_ref = refs
    for ref in arrived:
        place_arrived(ref, project_in_ref, ordered_ref, joint_ref, certain)


def front_kernel(
    arrived_ref,
    _ordered_ref,
    _joint_ref,
    segment_ref,
    query_mark_ref,
    key_mark_ref,
    project_in_ref,
    project_out_ref,
    slot_keys_ref,
    ordered_ref,
    joint_ref,
    hidden_ref,
    moe_normed_ref,
    slot_in_ref,
    context_ref,
    *,
    certain,
):
    tok_count, width = ordered_ref.shape
    place_arrived(arrived_ref, project_in_ref, ordered_ref, joint_ref, certain)

    lane = lax.broadcasted_iota(jnp.int32, (1, LANES), 1)
    first = lane < HEAD
    zero = jnp.zeros((), jnp.bfloat16)
    ones = jnp.ones((tok_count, LANES), jnp.bfloat16)
    scale = HEAD ** (-0.5) * math.log2(math.e)
    for pair in range(width // LANES):
        at = pair * LANES
        query = joint_ref[:, at : at + LANES]
        key = joint_ref[:, width + at : width + at + LANES]
        value = joint_ref[:, 2 * width + at : 2 * width + at + LANES]
        keys = jnp.concatenate([key, key_mark_ref[...]], axis=1)
        values = jnp.concatenate([value, ones], axis=1)
        parts = []
        for keep in (first, ~first):
            queries = jnp.concatenate(
                [jnp.where(keep, query, zero), query_mark_ref[...]], axis=1
            )
            scores = dot(queries, keys, ((1,), (1,)))
            top = jnp.max(scores, axis=1, keepdims=True)
            raised = jnp.exp2((scores - top) * scale).astype(jnp.bfloat16)
            parts.append(dot(raised, values))
        picked = jnp.where(first, parts[0][:, :LANES], parts[1][:, :LANES])
        total = jnp.where(first, parts[0][:, LANES:], parts[1][:, LANES:])
        context_ref[:, at : at + LANES] = (picked / total).astype(jnp.bfloat16)

    chunk = LANES
    made = None
    for start in [*range(0, tok_count, chunk), None]:
        following = None
        if start is not None:
            at = slice(start, start + chunk)
            following = at, dot(context_ref[at, :], project_out_ref[...])
        if made is not None:
            at, projected = made
            hidden = (ordered_ref[at, :].astype(jnp.float32) + projected).astype(jnp.bfloat16)
            hidden_ref[at, :] = hidden
            moe_normed_ref[at, :] = layer_norm(hidden.astype(jnp.float32)).astype(jnp.bfloat16)
        made = following
    moe_normed = moe_normed_ref[...]
    logits = dot(slot_keys_ref[...], moe_normed, ((1,), (1,)))
    blk_count = slot_in_ref.shape[1]
    column_image = lax.broadcasted_iota(jnp.int32, (logits.shape[0], 1), 0) % blk_count
    member = segment_ref[...] % blk_count == column_image
    top = jnp.max(jnp.where(member, logits, NEGATIVE), axis=1, keepdims=True)
    raised = jnp.where(member, jnp.exp(logits - top), 0.0)
    dispatch = raised / jnp.sum(raised, axis=1, keepdims=True)
    slot_in = dot(dispatch.astype(jnp.bfloat16), moe_normed)
    slot_in_ref[...] = slot_in.astype(jnp.bfloat16).reshape(slot_in_ref.shape)


def weigh_kernel(moe_normed_ref, slot_keys_ref, image_ref, combine_ref, *, blk_count):
    logits = dot(moe_normed_ref[...], slot_keys_ref[...], ((1,), (1,)))
    lane = lax.broadcasted_iota(jnp.int32, (1, LANES), 1)
    image_here = image_ref[...] == (lane % blk_count).astype(jnp.float32)
    member = jnp.concatenate([image_here] * (logits.shape[1] // LANES), axis=1)
    top = jnp.max(logits, axis=1, keepdims=True)
    raised = jnp.where(member, jnp.exp(logits - top), 0.0)
    combine = raised / jnp.sum(raised, axis=1, keepdims=True)
    combine_ref[...] = combine.astype(jnp.bfloat16)


def expert_kernel(arrived_ref, expert_in_ref, expert_out_ref, produced_ref, total_ref):
    rows, width = total_ref.shape
    slots = arrived_ref[...].reshape(rows, width)
    hidden_width = expert_in_ref.shape[2]
    step = math.gcd(hidden_width, 768)
    for at in range(0, hidden_width, step):
        inner = dot(slots, expert_in_ref[0, :, at : at + step])
        inner = 0.5 * inner * (1.0 + lax.erf(inner * math.sqrt(0.5)))
        part = dot(inner.astype(jnp.bfloat16), expert_out_ref[0, at : at + step, :])
        total_ref[...] = part if at == 0 else total_ref[...] + part
    produced_ref[...] = total_ref[...].astype(jnp.bfloat16).reshape(produced_ref.shape)


def combine_kernel(hidden_ref, combine_ref, returned_ref, out_ref):
    returned = returned_ref[...].reshape(combine_ref.shape[1], hidden_ref.shape[1])
    mixture = dot(combine_ref[...], returned)
    out_ref[...] = (hidden_ref[...].astype(jnp.float32) + mixture).astype(jnp.bfloat16)


def resident(*arrays, memory_space=pltpu.VMEM):
    return [pltpu.with_memory_space_constraint(array, memory_space) for array in arrays]


def whole(memory_space=pltpu.VMEM):
    return pl.BlockSpec(memory_space=memory_space)


def per_device(
    patches,
    owner_slot,
    segment_ids,
    block_mask,
    project_in,
    project_out,
    slot_keys,
    expert_in,
    expert_out,
):
    tok_count, width = patches.shape
    blk_count = owner_slot.shape[0]
    rows = tok_count // blk_count
    data_count = lax.axis_size("dp")
    column_count = lax.axis_size("expert")
    expert_count = slot_keys.shape[1]
    columns = expert_count * blk_count
    certain = data_count == blk_count
    params = pltpu.CompilerParams(vmem_limit_bytes=VMEM_LIMIT)

    flips = [*range(2, data_count), 1]
    sends = pl.pallas_call(
        functools.partial(send_kernel, flips=flips, columns=column_count),
        out_shape=[pltpu.VMEM((rows + TAG_ROWS, width), jnp.bfloat16)] * len(flips),
        in_specs=[whole(pltpu.SMEM), whole(pltpu.HBM)],
        out_specs=[whole()] * len(flips),
        scratch_shapes=[pltpu.SemaphoreType.DMA((len(flips),))],
        compiler_params=params,
        name="send",
    )(*resident(owner_slot, patches, memory_space=pltpu.HBM))
    arrived = [
        lax.ppermute(send, "dp", [(i, i ^ flip) for i in range(data_count)])
        for flip, send in zip(flips, sends)
    ]
    far, near = arrived[:-1], arrived[-1]

    (segment,) = resident(segment_ids.reshape(1, tok_count))
    streamed = [project_in, project_out, expert_in, expert_out]
    prepared = pl.pallas_call(
        functools.partial(prepare_kernel, columns=column_count, certain=certain),
        out_shape=[pltpu.VMEM(w.shape, w.dtype) for w in streamed]
        + [
            pltpu.VMEM((tok_count, LANES), jnp.bfloat16),
            pltpu.VMEM((tok_count, LANES), jnp.bfloat16),
            pltpu.VMEM((tok_count, LANES), jnp.float32),
            pltpu.VMEM((columns, width), jnp.bfloat16),
            pltpu.VMEM((tok_count, width), jnp.bfloat16),
            pltpu.VMEM((tok_count, 3 * width), jnp.bfloat16),
        ],
        in_specs=[whole(pltpu.SMEM)] * 2
        + [whole()] * 2
        + [whole(pltpu.HBM), whole()]
        + [whole(pltpu.HBM)] * len(streamed),
        out_specs=[whole()] * (len(streamed) + 6),
        scratch_shapes=[
            pltpu.VMEM((rows, width), jnp.bfloat16),
            pltpu.SemaphoreType.DMA((len(streamed) + 1,)),
        ],
        compiler_params=params,
        name="prepare",
    )(
        *resident(owner_slot, block_mask, memory_space=pltpu.HBM),
        segment,
        slot_keys,
        *resident(patches, memory_space=pltpu.HBM),
        *resident(near),
        *resident(*streamed, memory_space=pltpu.HBM),
    )
    project_in, project_out, expert_in, expert_out = prepared[:4]
    query_mark, key_mark, image, slot_keys_wide = prepared[4:8]
    placed = prepared[8:]

    placed_shapes = tuple(pltpu.VMEM(array.shape, array.dtype) for array in placed)
    *earlier, last = far
    if earlier:
        base = len(earlier) + 1
        placed = pl.pallas_call(
            functools.partial(middle_kernel, certain=certain),
            out_shape=placed_shapes,
            in_specs=[whole()] * (base + 2),
            out_specs=(whole(),) * 2,
            input_output_aliases={base + n: n for n in range(2)},
            compiler_params=params,
            name="middle",
        )(*resident(*earlier, project_in, *placed))
    *_, hidden, moe_normed, slot_in = pl.pallas_call(
        functools.partial(front_kernel, certain=certain),
        out_shape=(
            *placed_shapes,
            pltpu.VMEM((tok_count, width), jnp.bfloat16),
            pltpu.VMEM((tok_count, width), jnp.bfloat16),
            pltpu.VMEM((expert_count, blk_count, width), jnp.bfloat16),
        ),
        in_specs=[whole()] * 9,
        out_specs=(whole(),) * 5,
        input_output_aliases={1 + n: n for n in range(2)},
        scratch_shapes=[pltpu.VMEM((tok_count, width), jnp.bfloat16)],
        compiler_params=params,
        name="front",
    )(
        *resident(
            last,
            *placed,
            segment,
            query_mark,
            key_mark,
            project_in,
            project_out,
            slot_keys_wide,
        )
    )
    slots_here = lax.all_to_all(slot_in, AXES, split_axis=0, concat_axis=0, tiled=True)
    combine = pl.pallas_call(
        functools.partial(weigh_kernel, blk_count=blk_count),
        out_shape=pltpu.VMEM((tok_count, columns), jnp.bfloat16),
        in_specs=[whole()] * 3,
        out_specs=whole(),
        compiler_params=params,
        name="weigh",
    )(*resident(moe_normed, slot_keys_wide, image))
    produced = pl.pallas_call(
        expert_kernel,
        out_shape=pltpu.VMEM(slots_here.shape, jnp.bfloat16),
        in_specs=[whole()] * 3,
        out_specs=whole(),
        scratch_shapes=[pltpu.VMEM((columns, width), jnp.float32)],
        compiler_params=params,
        name="expert",
    )(*resident(slots_here, expert_in, expert_out))
    returned = lax.all_to_all(produced, AXES, split_axis=0, concat_axis=0, tiled=True)
    return pl.pallas_call(
        combine_kernel,
        out_shape=jax.ShapeDtypeStruct((tok_count, width), jnp.bfloat16),
        in_specs=[whole()] * 3,
        out_specs=whole(),
        compiler_params=params,
        name="combine",
    )(*resident(hidden, combine, returned))


def solution(mesh):
    in_specs = (
        P(AXES, None),
        P(AXES),
        P(AXES),
        P(AXES, None),
        P(),
        P(),
        P(),
        P(AXES, None, None),
        P(AXES, None, None),
    )
    return jax.shard_map(
        per_device, mesh=mesh, in_specs=in_specs, out_specs=P(AXES, None), check_vma=False
    )
```

```python
import functools
import math

import jax
import jax.numpy as jnp
from jax import lax
from jax.experimental import pallas as pl
from jax.experimental.pallas import tpu as pltpu
from jax.sharding import PartitionSpec as P


HEAD = 64
LANES = 128
SUBLANES = 8
EPS = 1e-06
NEGATIVE = -1e30
AXES = ("dp", "expert")
VMEM_LIMIT = 24 << 20


def layer_norm(values):
    centred = values - jnp.mean(values, axis=-1, keepdims=True)
    variance = jnp.mean(centred * centred, axis=-1, keepdims=True)
    return centred * lax.rsqrt(variance + EPS)


def dot(a, b, dims=((1,), (0,))):
    return lax.dot_general(a, b, (dims, ((), ())), preferred_element_type=jnp.float32)


def far_first(count):
    return [*range(2, count), 1]


def route_of(owner_ref, target, columns):
    blk_count = owner_ref.shape[0]
    source = jnp.int32(0)
    place = jnp.int32(-1)
    for block in range(blk_count):
        owner = owner_ref[block]
        hit = owner // (blk_count * columns) == target
        source = jnp.where(hit, block, source)
        place = jnp.where(hit, owner % blk_count, place)
    return source, place


def packed(block):
    rows, width = block.shape
    tiles = [
        block[:, at : at + LANES].reshape(rows // SUBLANES, SUBLANES, LANES)
        for at in range(0, width, LANES)
    ]
    return jnp.concatenate(tiles, axis=0).astype(jnp.bfloat16)


def unpacked(tiles, width):
    count = tiles.shape[0] * LANES // width
    parts = [
        tiles[at : at + count].reshape(count * SUBLANES, LANES)
        for at in range(0, tiles.shape[0], count)
    ]
    return jnp.concatenate(parts, axis=1)


def send_kernel(owner_ref, patches_ref, *refs, flips, columns):
    sends, own_ref = refs[:-1], refs[-1]
    rows = own_ref.shape[0]
    me = lax.axis_index("dp")

    def chosen(flip):
        source, place = route_of(owner_ref, me ^ flip, columns)
        return patches_ref[pl.ds(pl.multiple_of(source * rows, rows), rows), :], place

    for flip, send in zip(flips, sends):
        block, place = chosen(flip)
        tiles = send.shape[0] - 1
        send[:tiles] = packed(block.astype(jnp.float32))
        tag = jnp.full((1, SUBLANES, LANES), place.astype(jnp.float32))
        send[tiles : tiles + 1] = tag.astype(jnp.bfloat16)
    own_ref[...] = chosen(0)[0]


def place_block(block, place, project_in_ref, ordered_ref, joint_ref):
    rows = block.shape[0]
    at = pl.ds(pl.multiple_of(place * rows, rows), rows)
    ordered_ref[at, :] = block.astype(jnp.bfloat16)
    normed = layer_norm(block).astype(jnp.bfloat16)
    joint_ref[at, :] = dot(normed, project_in_ref[...]).astype(jnp.bfloat16)


def place_arrived(ref, project_in_ref, ordered_ref, joint_ref, certain):
    tiles = ref.shape[0] - 1
    place = jnp.max(ref[tiles].astype(jnp.float32)).astype(jnp.int32)

    def fill():
        block = unpacked(ref[:tiles].astype(jnp.float32), ordered_ref.shape[1])
        place_block(block, place, project_in_ref, ordered_ref, joint_ref)

    if certain:
        fill()
    else:
        pl.when(place >= 0)(fill)


def prepare_kernel(
    owner_ref,
    block_mask_ref,
    segment_ref,
    slot_keys_ref,
    own_ref,
    near_ref,
    *refs,
    columns,
    certain,
):
    count = (len(refs) - 6) // 2
    sources, weights = refs[:count], refs[count : 2 * count]
    query_mark_ref, key_mark_ref, slot_keys_wide_ref = refs[2 * count : 2 * count + 3]
    ordered_ref, joint_ref, sems = refs[2 * count + 3 :]
    blk_count = owner_ref.shape[0]
    tok_count = ordered_ref.shape[0]
    rows = own_ref.shape[0]
    copies = [
        pltpu.make_async_copy(source, weight, sems.at[n])
        for n, (source, weight) in enumerate(zip(sources, weights))
    ]
    _, place = route_of(owner_ref, lax.axis_index("dp"), columns)
    for copy in copies:
        copy.start()

    lane = lax.broadcasted_iota(jnp.int32, (1, LANES), 1)
    lane_float = lane.astype(jnp.float32)
    image = (segment_ref[...] % blk_count).astype(jnp.float32)
    image = jnp.transpose(jnp.broadcast_to(image, (LANES, tok_count)))
    image_is = image == lane_float
    for block in range(blk_count):
        at = slice(block * rows, (block + 1) * rows)
        blocked = jnp.zeros((1, LANES), jnp.float32)
        for other in range(blk_count):
            value = jnp.where(block_mask_ref[block, other] == 1, 0.0, NEGATIVE)
            blocked = jnp.where(lane == blk_count + other, value, blocked)
        query_mark_ref[at, :] = jnp.where(image_is[at], NEGATIVE, blocked).astype(jnp.bfloat16)
        block_is = jnp.where(lane == blk_count + block, 1.0, 0.0)
        key_mark_ref[at, :] = jnp.where(
            lane < blk_count, jnp.where(image_is[at], 0.0, 1.0), block_is
        ).astype(jnp.bfloat16)
    wide, experts = slot_keys_wide_ref.shape[0], slot_keys_ref.shape[1]
    column = lax.broadcasted_iota(jnp.int32, (wide, experts), 0)
    expert = lax.broadcasted_iota(jnp.int32, (wide, experts), 1)
    spread = jnp.where(column // blk_count == expert, 1.0, 0.0).astype(jnp.bfloat16)
    slot_keys_wide_ref[...] = dot(spread, slot_keys_ref[...], ((1,), (1,))).astype(jnp.bfloat16)

    copies[0].wait()
    project_in_ref = weights[0]
    place_block(own_ref[...].astype(jnp.float32), place, project_in_ref, ordered_ref, joint_ref)
    place_arrived(near_ref, project_in_ref, ordered_ref, joint_ref, certain)
    for copy in copies[1:]:
        copy.wait()


def middle_kernel(*refs, certain):
    *arrived, project_in_ref, _, _, ordered_ref, joint_ref = refs
    for ref in arrived:
        place_arrived(ref, project_in_ref, ordered_ref, joint_ref, certain)


def front_kernel(
    arrived_ref,
    _ordered_ref,
    _joint_ref,
    segment_ref,
    query_mark_ref,
    key_mark_ref,
    project_in_ref,
    project_out_ref,
    slot_keys_ref,
    expert_in_hbm,
    expert_out_hbm,
    ordered_ref,
    joint_ref,
    hidden_ref,
    slot_in_ref,
    combine_ref,
    expert_in_ref,
    expert_out_ref,
    context_ref,
    sems,
    *,
    certain,
):
    tok_count, width = ordered_ref.shape
    copies = [
        pltpu.make_async_copy(expert_in_hbm, expert_in_ref, sems.at[0]),
        pltpu.make_async_copy(expert_out_hbm, expert_out_ref, sems.at[1]),
    ]
    for copy in copies:
        copy.start()
    place_arrived(arrived_ref, project_in_ref, ordered_ref, joint_ref, certain)

    lane = lax.broadcasted_iota(jnp.int32, (1, LANES), 1)
    first = lane < HEAD
    zero = jnp.zeros((), jnp.bfloat16)
    ones = jnp.ones((tok_count, LANES), jnp.bfloat16)
    scale = HEAD ** (-0.5) * math.log2(math.e)
    for pair in range(width // LANES):
        at = pair * LANES
        query = joint_ref[:, at : at + LANES]
        key = joint_ref[:, width + at : width + at + LANES]
        value = joint_ref[:, 2 * width + at : 2 * width + at + LANES]
        keys = jnp.concatenate([key, key_mark_ref[...]], axis=1)
        values = jnp.concatenate([value, ones], axis=1)
        parts = []
        for keep in (first, ~first):
            queries = jnp.concatenate(
                [jnp.where(keep, query, zero), query_mark_ref[...]], axis=1
            )
            scores = dot(queries, keys, ((1,), (1,)))
            top = jnp.max(scores, axis=1, keepdims=True)
            raised = jnp.exp2((scores - top) * scale).astype(jnp.bfloat16)
            parts.append(dot(raised, values))
        picked = jnp.where(first, parts[0][:, :LANES], parts[1][:, :LANES])
        total = jnp.where(first, parts[0][:, LANES:], parts[1][:, LANES:])
        context_ref[:, at : at + LANES] = (picked / total).astype(jnp.bfloat16)

    hidden = (
        ordered_ref[...].astype(jnp.float32) + dot(context_ref[...], project_out_ref[...])
    ).astype(jnp.bfloat16)
    hidden_ref[...] = hidden
    moe_normed = layer_norm(hidden.astype(jnp.float32)).astype(jnp.bfloat16)
    logits = dot(slot_keys_ref[...], moe_normed, ((1,), (1,)))
    blk_count = slot_in_ref.shape[1]
    column_image = lax.broadcasted_iota(jnp.int32, (logits.shape[0], 1), 0) % blk_count
    member = segment_ref[...] % blk_count == column_image
    top = jnp.max(jnp.where(member, logits, NEGATIVE), axis=1, keepdims=True)
    raised = jnp.where(member, jnp.exp(logits - top), 0.0)
    dispatch = raised / jnp.sum(raised, axis=1, keepdims=True)
    slot_in = dot(dispatch.astype(jnp.bfloat16), moe_normed)
    slot_in_ref[...] = slot_in.astype(jnp.bfloat16).reshape(slot_in_ref.shape)
    top = jnp.max(logits, axis=0, keepdims=True)
    raised = jnp.where(member, jnp.exp(logits - top), 0.0)
    combine = raised / jnp.sum(raised, axis=0, keepdims=True)
    combine_ref[...] = jnp.transpose(combine.astype(jnp.bfloat16))
    for copy in copies:
        copy.wait()


def expert_kernel(arrived_ref, expert_in_ref, expert_out_ref, produced_ref, total_ref):
    rows, width = total_ref.shape
    slots = arrived_ref[...].reshape(rows, width)
    hidden_width = expert_in_ref.shape[2]
    step = math.gcd(hidden_width, 768)
    for at in range(0, hidden_width, step):
        inner = dot(slots, expert_in_ref[0, :, at : at + step])
        inner = 0.5 * inner * (1.0 + lax.erf(inner * math.sqrt(0.5)))
        part = dot(inner.astype(jnp.bfloat16), expert_out_ref[0, at : at + step, :])
        total_ref[...] = part if at == 0 else total_ref[...] + part
    produced_ref[...] = total_ref[...].astype(jnp.bfloat16).reshape(produced_ref.shape)


def combine_kernel(hidden_ref, combine_ref, returned_ref, out_hbm, out_ref, sems):
    returned = returned_ref[...].reshape(combine_ref.shape[1], hidden_ref.shape[1])
    count = sems.shape[0]
    rows = hidden_ref.shape[0] // count
    copies = []
    for n in range(count):
        at = slice(n * rows, (n + 1) * rows)
        mixture = dot(combine_ref[at, :], returned)
        out_ref[at, :] = (hidden_ref[at, :].astype(jnp.float32) + mixture).astype(jnp.bfloat16)
        copies.append(pltpu.make_async_copy(out_ref.at[at, :], out_hbm.at[at, :], sems.at[n]))
        copies[-1].start()
    for copy in copies:
        copy.wait()


def resident(*arrays, memory_space=pltpu.VMEM):
    return [pltpu.with_memory_space_constraint(array, memory_space) for array in arrays]


def whole(memory_space=pltpu.VMEM):
    return pl.BlockSpec(memory_space=memory_space)


def per_device(
    patches,
    owner_slot,
    segment_ids,
    block_mask,
    project_in,
    project_out,
    slot_keys,
    expert_in,
    expert_out,
):
    tok_count, width = patches.shape
    blk_count = owner_slot.shape[0]
    rows = tok_count // blk_count
    data_count = lax.axis_size("dp")
    column_count = lax.axis_size("expert")
    expert_count = slot_keys.shape[1]
    columns = expert_count * blk_count
    certain = data_count == blk_count
    params = pltpu.CompilerParams(vmem_limit_bytes=VMEM_LIMIT)

    flips = far_first(data_count)
    tiles = rows * width // (SUBLANES * LANES)
    *sends, own = pl.pallas_call(
        functools.partial(send_kernel, flips=flips, columns=column_count),
        out_shape=[pltpu.VMEM((tiles + 1, SUBLANES, LANES), jnp.bfloat16)] * len(flips)
        + [pltpu.VMEM((rows, width), jnp.bfloat16)],
        in_specs=[whole(pltpu.SMEM), whole()],
        out_specs=[whole()] * (len(flips) + 1),
        compiler_params=params,
        name="send",
    )(*resident(owner_slot, patches, memory_space=pltpu.HBM))
    arrived = []
    for flip, send in zip(flips, sends):
        arrived.append(lax.ppermute(send, "dp", [(i, i ^ flip) for i in range(data_count)]))
    far, near = arrived[:-1], arrived[-1]

    segment = segment_ids.reshape(1, tok_count)
    streamed = [project_in, project_out]
    prepared = pl.pallas_call(
        functools.partial(prepare_kernel, columns=column_count, certain=certain),
        out_shape=[pltpu.VMEM(w.shape, w.dtype) for w in streamed]
        + [
            pltpu.VMEM((tok_count, LANES), jnp.bfloat16),
            pltpu.VMEM((tok_count, LANES), jnp.bfloat16),
            pltpu.VMEM((columns, width), jnp.bfloat16),
            pltpu.VMEM((tok_count, width), jnp.bfloat16),
            pltpu.VMEM((tok_count, 3 * width), jnp.bfloat16),
        ],
        in_specs=[whole(pltpu.SMEM)] * 2
        + [whole()] * 4
        + [whole(pltpu.HBM)] * len(streamed),
        out_specs=[whole()] * (len(streamed) + 5),
        scratch_shapes=[pltpu.SemaphoreType.DMA((len(streamed),))],
        compiler_params=params,
        name="prepare",
    )(
        *resident(owner_slot, block_mask, segment, slot_keys, memory_space=pltpu.HBM),
        *resident(own, near),
        *resident(*streamed, memory_space=pltpu.HBM),
    )
    project_in, project_out = prepared[:2]
    query_mark, key_mark, slot_keys_wide = prepared[2:5]
    placed = prepared[5:]

    placed_shapes = tuple(pltpu.VMEM(array.shape, array.dtype) for array in placed)
    *earlier, last = far
    if earlier:
        base = len(earlier) + 1
        placed = pl.pallas_call(
            functools.partial(middle_kernel, certain=certain),
            out_shape=placed_shapes,
            in_specs=[whole()] * (base + 2),
            out_specs=(whole(),) * 2,
            input_output_aliases={base + n: n for n in range(2)},
            compiler_params=params,
            name="middle",
        )(*resident(*earlier, project_in, *placed))
    *_, hidden, slot_in, combine, expert_in, expert_out = pl.pallas_call(
        functools.partial(front_kernel, certain=certain),
        out_shape=(
            *placed_shapes,
            pltpu.VMEM((tok_count, width), jnp.bfloat16),
            pltpu.VMEM((expert_count, blk_count, width), jnp.bfloat16),
            pltpu.VMEM((tok_count, columns), jnp.bfloat16),
            pltpu.VMEM(expert_in.shape, jnp.bfloat16),
            pltpu.VMEM(expert_out.shape, jnp.bfloat16),
        ),
        in_specs=[whole()] * 9 + [whole(pltpu.HBM)] * 2,
        out_specs=(whole(),) * 7,
        input_output_aliases={1 + n: n for n in range(2)},
        scratch_shapes=[
            pltpu.VMEM((tok_count, width), jnp.bfloat16),
            pltpu.SemaphoreType.DMA((2,)),
        ],
        compiler_params=params,
        name="front",
    )(
        *resident(last, *placed),
        *resident(segment, memory_space=pltpu.HBM),
        *resident(query_mark, key_mark, project_in, project_out, slot_keys_wide),
        *resident(expert_in, expert_out, memory_space=pltpu.HBM),
    )
    slots_here = lax.all_to_all(slot_in, AXES, split_axis=0, concat_axis=0, tiled=True)
    produced = pl.pallas_call(
        expert_kernel,
        out_shape=pltpu.VMEM(slots_here.shape, jnp.bfloat16),
        in_specs=[whole()] * 3,
        out_specs=whole(),
        scratch_shapes=[pltpu.VMEM((columns, width), jnp.float32)],
        compiler_params=params,
        name="expert",
    )(*resident(slots_here, expert_in, expert_out))
    returned = lax.all_to_all(produced, AXES, split_axis=0, concat_axis=0, tiled=True)
    return pl.pallas_call(
        combine_kernel,
        out_shape=jax.ShapeDtypeStruct((tok_count, width), jnp.bfloat16),
        in_specs=[whole()] * 3,
        out_specs=whole(pltpu.HBM),
        scratch_shapes=[
            pltpu.VMEM((tok_count, width), jnp.bfloat16),
            pltpu.SemaphoreType.DMA((blk_count,)),
        ],
        compiler_params=params,
        name="combine",
    )(*resident(hidden, combine, returned))


def solution(mesh):
    in_specs = (
        P(AXES, None),
        P(AXES),
        P(AXES),
        P(AXES, None),
        P(),
        P(),
        P(),
        P(AXES, None, None),
        P(AXES, None, None),
    )
    return jax.shard_map(
        per_device,
        mesh=mesh,
        in_specs=in_specs,
        out_specs=P(AXES, None),
        check_vma=False,
    )
```

```python
import functools
import math

import jax
import jax.numpy as jnp
from jax import lax
from jax.experimental import pallas as pl
from jax.experimental.pallas import tpu as pltpu
from jax.sharding import PartitionSpec as P


HEAD = 64
LANES = 128
SUBLANES = 8
EPS = 1e-06
NEGATIVE = -1e30
AXES = ("dp", "expert")
VMEM_LIMIT = 24 << 20


def layer_norm(values):
    centred = values - jnp.mean(values, axis=-1, keepdims=True)
    variance = jnp.mean(centred * centred, axis=-1, keepdims=True)
    return centred * lax.rsqrt(variance + EPS)


def dot(a, b, dims=((1,), (0,))):
    return lax.dot_general(a, b, (dims, ((), ())), preferred_element_type=jnp.float32)


def far_first(count):
    return [*range(2, count), 1]


def route_of(owner_ref, target, columns):
    blk_count = owner_ref.shape[0]
    source = jnp.int32(0)
    place = jnp.int32(-1)
    for block in range(blk_count):
        owner = owner_ref[block]
        hit = owner // (blk_count * columns) == target
        source = jnp.where(hit, block, source)
        place = jnp.where(hit, owner % blk_count, place)
    return source, place


def packed(block):
    rows, width = block.shape
    tiles = [
        block[:, at : at + LANES].reshape(rows // SUBLANES, SUBLANES, LANES)
        for at in range(0, width, LANES)
    ]
    return jnp.concatenate(tiles, axis=0).astype(jnp.bfloat16)


def unpacked(tiles, width):
    count = tiles.shape[0] * LANES // width
    parts = [
        tiles[at : at + count].reshape(count * SUBLANES, LANES)
        for at in range(0, tiles.shape[0], count)
    ]
    return jnp.concatenate(parts, axis=1)


def send_kernel(owner_ref, patches_ref, *refs, flips, columns):
    sends, own_ref = refs[:-1], refs[-1]
    rows = own_ref.shape[0]
    me = lax.axis_index("dp")

    def chosen(flip):
        source, place = route_of(owner_ref, me ^ flip, columns)
        return patches_ref[pl.ds(pl.multiple_of(source * rows, rows), rows), :], place

    for flip, send in zip(flips, sends):
        block, place = chosen(flip)
        tiles = send.shape[0] - 1
        send[:tiles] = packed(block.astype(jnp.float32))
        tag = jnp.full((1, SUBLANES, LANES), place.astype(jnp.float32))
        send[tiles : tiles + 1] = tag.astype(jnp.bfloat16)
    own_ref[...] = chosen(0)[0]


def place_block(block, place, project_in_ref, ordered_ref, joint_ref):
    rows = block.shape[0]
    at = pl.ds(pl.multiple_of(place * rows, rows), rows)
    ordered_ref[at, :] = block.astype(jnp.bfloat16)
    normed = layer_norm(block).astype(jnp.bfloat16)
    joint_ref[at, :] = dot(normed, project_in_ref[...]).astype(jnp.bfloat16)


def place_arrived(ref, project_in_ref, ordered_ref, joint_ref, certain):
    tiles = ref.shape[0] - 1
    place = jnp.max(ref[tiles].astype(jnp.float32)).astype(jnp.int32)

    def fill():
        block = unpacked(ref[:tiles].astype(jnp.float32), ordered_ref.shape[1])
        place_block(block, place, project_in_ref, ordered_ref, joint_ref)

    if certain:
        fill()
    else:
        pl.when(place >= 0)(fill)


def prepare_kernel(
    owner_ref,
    block_mask_ref,
    segment_ref,
    slot_keys_ref,
    own_ref,
    near_ref,
    project_in_hbm,
    project_out_hbm,
    project_in_ref,
    project_out_ref,
    image_ref,
    query_mark_ref,
    key_mark_ref,
    slot_keys_wide_ref,
    ordered_ref,
    joint_ref,
    sems,
    *,
    columns,
    certain,
):
    blk_count = owner_ref.shape[0]
    tok_count = ordered_ref.shape[0]
    rows = own_ref.shape[0]
    copies = [
        pltpu.make_async_copy(project_in_hbm, project_in_ref, sems.at[0]),
        pltpu.make_async_copy(project_out_hbm, project_out_ref, sems.at[1]),
    ]
    for copy in copies:
        copy.start()
    _, place = route_of(owner_ref, lax.axis_index("dp"), columns)

    lane = lax.broadcasted_iota(jnp.int32, (1, LANES), 1)
    lane_float = lane.astype(jnp.float32)
    image = segment_ref[...] % blk_count
    image_ref[...] = image
    image = image.astype(jnp.float32)
    image = jnp.transpose(jnp.broadcast_to(image, (LANES, tok_count)))
    image_is = image == lane_float
    for block in range(blk_count):
        at = slice(block * rows, (block + 1) * rows)
        blocked = jnp.zeros((1, LANES), jnp.float32)
        for other in range(blk_count):
            value = jnp.where(block_mask_ref[block, other] == 1, 0.0, NEGATIVE)
            blocked = jnp.where(lane == blk_count + other, value, blocked)
        query_mark_ref[at, :] = jnp.where(image_is[at], NEGATIVE, blocked).astype(jnp.bfloat16)
        block_is = jnp.where(lane == blk_count + block, 1.0, 0.0)
        key_mark_ref[at, :] = jnp.where(
            lane < blk_count, jnp.where(image_is[at], 0.0, 1.0), block_is
        ).astype(jnp.bfloat16)
    wide, experts = slot_keys_wide_ref.shape[0], slot_keys_ref.shape[1]
    column = lax.broadcasted_iota(jnp.int32, (wide, experts), 0)
    expert = lax.broadcasted_iota(jnp.int32, (wide, experts), 1)
    spread = jnp.where(column // blk_count == expert, 1.0, 0.0).astype(jnp.bfloat16)
    slot_keys_wide_ref[...] = dot(spread, slot_keys_ref[...], ((1,), (1,))).astype(jnp.bfloat16)

    copies[0].wait()
    place_block(own_ref[...].astype(jnp.float32), place, project_in_ref, ordered_ref, joint_ref)
    place_arrived(near_ref, project_in_ref, ordered_ref, joint_ref, certain)
    copies[1].wait()


def middle_kernel(*refs, certain):
    *arrived, project_in_ref, _, _, ordered_ref, joint_ref = refs
    for ref in arrived:
        place_arrived(ref, project_in_ref, ordered_ref, joint_ref, certain)


def front_kernel(
    arrived_ref,
    _ordered_ref,
    _joint_ref,
    image_ref,
    query_mark_ref,
    key_mark_ref,
    project_in_ref,
    project_out_ref,
    slot_keys_ref,
    expert_in_hbm,
    expert_out_hbm,
    ordered_ref,
    joint_ref,
    hidden_ref,
    slot_in_ref,
    combine_ref,
    expert_in_ref,
    expert_out_ref,
    context_ref,
    sems,
    *,
    certain,
):
    tok_count, width = ordered_ref.shape
    copies = [
        pltpu.make_async_copy(expert_in_hbm, expert_in_ref, sems.at[0]),
        pltpu.make_async_copy(expert_out_hbm, expert_out_ref, sems.at[1]),
    ]
    for copy in copies:
        copy.start()
    place_arrived(arrived_ref, project_in_ref, ordered_ref, joint_ref, certain)

    lane = lax.broadcasted_iota(jnp.int32, (1, LANES), 1)
    first = lane < HEAD
    zero = jnp.zeros((), jnp.bfloat16)
    ones = jnp.ones((tok_count, LANES), jnp.bfloat16)
    scale = HEAD ** (-0.5) * math.log2(math.e)
    for pair in range(width // LANES):
        at = pair * LANES
        query = joint_ref[:, at : at + LANES]
        key = joint_ref[:, width + at : width + at + LANES]
        value = joint_ref[:, 2 * width + at : 2 * width + at + LANES]
        keys = jnp.concatenate([key, key_mark_ref[...]], axis=1)
        values = jnp.concatenate([value, ones], axis=1)
        parts = []
        for keep in (first, ~first):
            queries = jnp.concatenate(
                [jnp.where(keep, query, zero), query_mark_ref[...]], axis=1
            )
            scores = dot(queries, keys, ((1,), (1,)))
            top = jnp.max(scores, axis=1, keepdims=True)
            raised = jnp.exp2((scores - top) * scale).astype(jnp.bfloat16)
            parts.append(dot(raised, values))
        picked = jnp.where(first, parts[0][:, :LANES], parts[1][:, :LANES])
        total = jnp.where(first, parts[0][:, LANES:], parts[1][:, LANES:])
        context_ref[:, at : at + LANES] = (picked / total).astype(jnp.bfloat16)

    hidden = (
        ordered_ref[...].astype(jnp.float32) + dot(context_ref[...], project_out_ref[...])
    ).astype(jnp.bfloat16)
    hidden_ref[...] = hidden
    moe_normed = layer_norm(hidden.astype(jnp.float32)).astype(jnp.bfloat16)
    logits = dot(slot_keys_ref[...], moe_normed, ((1,), (1,)))
    blk_count = slot_in_ref.shape[1]
    column_image = lax.broadcasted_iota(jnp.int32, (logits.shape[0], 1), 0) % blk_count
    member = image_ref[...] == column_image
    top = jnp.max(jnp.where(member, logits, NEGATIVE), axis=1, keepdims=True)
    raised = jnp.where(member, jnp.exp(logits - top), 0.0)
    dispatch = raised / jnp.sum(raised, axis=1, keepdims=True)
    slot_in = dot(dispatch.astype(jnp.bfloat16), moe_normed)
    slot_in_ref[...] = slot_in.astype(jnp.bfloat16).reshape(slot_in_ref.shape)
    top = jnp.max(logits, axis=0, keepdims=True)
    raised = jnp.where(member, jnp.exp(logits - top), 0.0)
    combine = raised / jnp.sum(raised, axis=0, keepdims=True)
    combine_ref[...] = jnp.transpose(combine.astype(jnp.bfloat16))
    for copy in copies:
        copy.wait()


def expert_kernel(arrived_ref, expert_in_ref, expert_out_ref, produced_ref, total_ref):
    rows, width = total_ref.shape
    slots = arrived_ref[...].reshape(rows, width)
    hidden_width = expert_in_ref.shape[2]
    step = math.gcd(hidden_width, 768)
    for at in range(0, hidden_width, step):
        inner = dot(slots, expert_in_ref[0, :, at : at + step])
        inner = 0.5 * inner * (1.0 + lax.erf(inner * math.sqrt(0.5)))
        part = dot(inner.astype(jnp.bfloat16), expert_out_ref[0, at : at + step, :])
        total_ref[...] = part if at == 0 else total_ref[...] + part
    produced_ref[...] = total_ref[...].astype(jnp.bfloat16).reshape(produced_ref.shape)


def combine_kernel(hidden_ref, combine_ref, returned_ref, out_hbm, out_ref, sems):
    returned = returned_ref[...].reshape(combine_ref.shape[1], hidden_ref.shape[1])
    count = sems.shape[0]
    rows = hidden_ref.shape[0] // count
    copies = []
    for n in range(count):
        at = slice(n * rows, (n + 1) * rows)
        mixture = dot(combine_ref[at, :], returned)
        out_ref[at, :] = (hidden_ref[at, :].astype(jnp.float32) + mixture).astype(jnp.bfloat16)
        copies.append(pltpu.make_async_copy(out_ref.at[at, :], out_hbm.at[at, :], sems.at[n]))
        copies[-1].start()
    for copy in copies:
        copy.wait()


def resident(*arrays, memory_space=pltpu.VMEM):
    return [pltpu.with_memory_space_constraint(array, memory_space) for array in arrays]


def whole(memory_space=pltpu.VMEM):
    return pl.BlockSpec(memory_space=memory_space)


def per_device(
    patches,
    owner_slot,
    segment_ids,
    block_mask,
    project_in,
    project_out,
    slot_keys,
    expert_in,
    expert_out,
):
    tok_count, width = patches.shape
    blk_count = owner_slot.shape[0]
    rows = tok_count // blk_count
    data_count = lax.axis_size("dp")
    column_count = lax.axis_size("expert")
    expert_count = slot_keys.shape[1]
    columns = expert_count * blk_count
    certain = data_count == blk_count
    params = pltpu.CompilerParams(vmem_limit_bytes=VMEM_LIMIT)

    flips = far_first(data_count)
    tiles = rows * width // (SUBLANES * LANES)
    *sends, own = pl.pallas_call(
        functools.partial(send_kernel, flips=flips, columns=column_count),
        out_shape=[pltpu.VMEM((tiles + 1, SUBLANES, LANES), jnp.bfloat16)] * len(flips)
        + [pltpu.VMEM((rows, width), jnp.bfloat16)],
        in_specs=[whole(pltpu.SMEM), whole()],
        out_specs=[whole()] * (len(flips) + 1),
        compiler_params=params,
        name="send",
    )(*resident(owner_slot, patches, memory_space=pltpu.HBM))
    arrived = []
    for flip, send in zip(flips, sends):
        arrived.append(lax.ppermute(send, "dp", [(i, i ^ flip) for i in range(data_count)]))
    far, near = arrived[:-1], arrived[-1]

    segment = segment_ids.reshape(1, tok_count)
    prepared = pl.pallas_call(
        functools.partial(prepare_kernel, columns=column_count, certain=certain),
        out_shape=[
            pltpu.VMEM(project_in.shape, jnp.bfloat16),
            pltpu.VMEM(project_out.shape, jnp.bfloat16),
            pltpu.VMEM((1, tok_count), jnp.int32),
            pltpu.VMEM((tok_count, LANES), jnp.bfloat16),
            pltpu.VMEM((tok_count, LANES), jnp.bfloat16),
            pltpu.VMEM((columns, width), jnp.bfloat16),
            pltpu.VMEM((tok_count, width), jnp.bfloat16),
            pltpu.VMEM((tok_count, 3 * width), jnp.bfloat16),
        ],
        in_specs=[whole(pltpu.SMEM)] * 2 + [whole()] * 4 + [whole(pltpu.HBM)] * 2,
        out_specs=[whole()] * 8,
        scratch_shapes=[pltpu.SemaphoreType.DMA((2,))],
        compiler_params=params,
        name="prepare",
    )(
        *resident(owner_slot, block_mask, segment, slot_keys, memory_space=pltpu.HBM),
        *resident(own, near),
        *resident(project_in, project_out, memory_space=pltpu.HBM),
    )
    project_in, project_out, image, query_mark, key_mark, slot_keys_wide, *placed = prepared

    placed_shapes = tuple(pltpu.VMEM(array.shape, array.dtype) for array in placed)
    *earlier, last = far
    if earlier:
        base = len(earlier) + 1
        placed = pl.pallas_call(
            functools.partial(middle_kernel, certain=certain),
            out_shape=placed_shapes,
            in_specs=[whole()] * (base + 2),
            out_specs=(whole(),) * 2,
            input_output_aliases={base + n: n for n in range(2)},
            compiler_params=params,
            name="middle",
        )(*resident(*earlier, project_in, *placed))
    *_, hidden, slot_in, combine, expert_in, expert_out = pl.pallas_call(
        functools.partial(front_kernel, certain=certain),
        out_shape=(
            *placed_shapes,
            pltpu.VMEM((tok_count, width), jnp.bfloat16),
            pltpu.VMEM((expert_count, blk_count, width), jnp.bfloat16),
            pltpu.VMEM((tok_count, columns), jnp.bfloat16),
            pltpu.VMEM(expert_in.shape, jnp.bfloat16),
            pltpu.VMEM(expert_out.shape, jnp.bfloat16),
        ),
        in_specs=[whole()] * 9 + [whole(pltpu.HBM)] * 2,
        out_specs=(whole(),) * 7,
        input_output_aliases={1 + n: n for n in range(2)},
        scratch_shapes=[
            pltpu.VMEM((tok_count, width), jnp.bfloat16),
            pltpu.SemaphoreType.DMA((2,)),
        ],
        compiler_params=params,
        name="front",
    )(
        *resident(last, *placed, image, query_mark, key_mark),
        *resident(project_in, project_out, slot_keys_wide),
        *resident(expert_in, expert_out, memory_space=pltpu.HBM),
    )
    slots_here = lax.all_to_all(slot_in, AXES, split_axis=0, concat_axis=0, tiled=True)
    produced = pl.pallas_call(
        expert_kernel,
        out_shape=pltpu.VMEM(slots_here.shape, jnp.bfloat16),
        in_specs=[whole()] * 3,
        out_specs=whole(),
        scratch_shapes=[pltpu.VMEM((columns, width), jnp.float32)],
        compiler_params=params,
        name="expert",
    )(*resident(slots_here, expert_in, expert_out))
    returned = lax.all_to_all(produced, AXES, split_axis=0, concat_axis=0, tiled=True)
    return pl.pallas_call(
        combine_kernel,
        out_shape=jax.ShapeDtypeStruct((tok_count, width), jnp.bfloat16),
        in_specs=[whole()] * 3,
        out_specs=whole(pltpu.HBM),
        scratch_shapes=[
            pltpu.VMEM((tok_count, width), jnp.bfloat16),
            pltpu.SemaphoreType.DMA((blk_count,)),
        ],
        compiler_params=params,
        name="combine",
    )(*resident(hidden, combine, returned))


def solution(mesh):
    in_specs = (
        P(AXES, None),
        P(AXES),
        P(AXES),
        P(AXES, None),
        P(),
        P(),
        P(),
        P(AXES, None, None),
        P(AXES, None, None),
    )
    return jax.shard_map(
        per_device,
        mesh=mesh,
        in_specs=in_specs,
        out_specs=P(AXES, None),
        check_vma=False,
    )
```

```python
import functools
import math

import jax
import jax.numpy as jnp
from jax import lax
from jax.experimental import pallas as pl
from jax.experimental.pallas import tpu as pltpu
from jax.sharding import PartitionSpec as P


HEAD = 64
LANES = 128
SUBLANES = 8
EPS = 1e-06
NEGATIVE = -1e30
AXES = ("dp", "expert")
VMEM_LIMIT = 24 << 20


def layer_norm(values):
    centred = values - jnp.mean(values, axis=-1, keepdims=True)
    variance = jnp.mean(centred * centred, axis=-1, keepdims=True)
    return centred * lax.rsqrt(variance + EPS)


def dot(a, b, dims=((1,), (0,))):
    return lax.dot_general(a, b, (dims, ((), ())), preferred_element_type=jnp.float32)


def far_first(count):
    return [*range(2, count), 1]


def route_of(owner_ref, target, columns):
    blk_count = owner_ref.shape[0]
    source = jnp.int32(0)
    place = jnp.int32(-1)
    for block in range(blk_count):
        owner = owner_ref[block]
        hit = owner // (blk_count * columns) == target
        source = jnp.where(hit, block, source)
        place = jnp.where(hit, owner % blk_count, place)
    return source, place


def packed(block):
    rows, width = block.shape
    tiles = [
        block[:, at : at + LANES].reshape(rows // SUBLANES, SUBLANES, LANES)
        for at in range(0, width, LANES)
    ]
    return jnp.concatenate(tiles, axis=0).astype(jnp.bfloat16)


def unpacked(tiles, width):
    count = tiles.shape[0] * LANES // width
    parts = [
        tiles[at : at + count].reshape(count * SUBLANES, LANES)
        for at in range(0, tiles.shape[0], count)
    ]
    return jnp.concatenate(parts, axis=1)


def send_kernel(owner_ref, patches_ref, *refs, flips, columns):
    sends, own_ref = refs[:-1], refs[-1]
    rows = own_ref.shape[0]
    me = lax.axis_index("dp")

    def chosen(flip):
        source, place = route_of(owner_ref, me ^ flip, columns)
        return patches_ref[pl.ds(pl.multiple_of(source * rows, rows), rows), :], place

    for flip, send in zip(flips, sends):
        block, place = chosen(flip)
        tiles = send.shape[0] - 1
        send[:tiles] = packed(block.astype(jnp.float32))
        tag = jnp.full((1, SUBLANES, LANES), place.astype(jnp.float32))
        send[tiles : tiles + 1] = tag.astype(jnp.bfloat16)
    own_ref[...] = chosen(0)[0]


def block_at(index, rows):
    if isinstance(index, int):
        return slice(index * rows, (index + 1) * rows)
    return pl.ds(pl.multiple_of(index * rows, rows), rows)


def place_block(block, index, project_in_ref, ordered_ref, joint_ref):
    at = block_at(index, block.shape[0])
    ordered_ref[at, :] = block.astype(jnp.bfloat16)
    normed = layer_norm(block).astype(jnp.bfloat16)
    joint_ref[at, :] = dot(normed, project_in_ref[...]).astype(jnp.bfloat16)


def place_arrived(ref, slot, project_in_ref, ordered_ref, joint_ref):
    tiles = ref.shape[0] - 1
    place = jnp.max(ref[tiles].astype(jnp.float32)).astype(jnp.int32)

    def fill(index):
        block = unpacked(ref[:tiles].astype(jnp.float32), ordered_ref.shape[1])
        place_block(block, index, project_in_ref, ordered_ref, joint_ref)

    if slot is not None:
        fill(slot)
    else:
        pl.when(place >= 0)(lambda: fill(place))
    return place


def read_place(places_ref, slot):
    return jnp.max(places_ref[slot : slot + 1, :]).astype(jnp.int32)


def note_place(places_ref, slot, place):
    places_ref[slot : slot + 1, :] = jnp.full((1, LANES), place.astype(jnp.float32))


def gathered(mark_ref, places, rows):
    return jnp.concatenate([mark_ref[block_at(place, rows), :] for place in places], axis=0)


class Attention:
    def __init__(self, joint_ref, query_mark, key_mark):
        self.joint_ref, self.query_mark, self.key_mark = joint_ref, query_mark, key_mark
        self.width = joint_ref.shape[1] // 3
        self.scale = HEAD ** (-0.5) * math.log2(math.e)
        first = lax.broadcasted_iota(jnp.int32, (1, LANES), 1) < HEAD
        self.first, self.keeps = first, (first, ~first)
        self.zero = jnp.zeros((), jnp.bfloat16)

    def part(self, which, pair, rows):
        at = which * self.width + pair * LANES
        return self.joint_ref[rows, at : at + LANES]

    def begin(self, finish, pair, start, stop, keys_stop):
        query = self.part(0, pair, slice(start, stop))
        span = slice(0, keys_stop)
        keys = jnp.concatenate([self.part(1, pair, span), self.key_mark[span]], axis=1)
        ones = jnp.ones((keys_stop, LANES), jnp.bfloat16)
        values = jnp.concatenate([self.part(2, pair, span), ones], axis=1)
        scores = []
        for keep in self.keeps:
            queries = jnp.concatenate(
                [jnp.where(keep, query, self.zero), self.query_mark[start:stop]], axis=1
            )
            scores.append(dot(queries, keys, ((1,), (1,))))
        yield
        tops = [jnp.max(part, axis=1, keepdims=True) for part in scores]
        raised = [
            jnp.exp2((part - top) * self.scale).astype(jnp.bfloat16)
            for part, top in zip(scores, tops)
        ]
        yield
        parts = [dot(part, values) for part in raised]
        picked = jnp.where(self.first, parts[0][:, :LANES], parts[1][:, :LANES])
        total = jnp.where(self.first, parts[0][:, LANES:], parts[1][:, LANES:])
        finish(tops, picked, total)

    def extend(self, finish, pair, stop, block, old):
        queries = jnp.concatenate(
            [self.part(0, pair, slice(0, stop)), self.query_mark[:stop]], axis=1
        )
        key, value = self.part(1, pair, block), self.part(2, pair, block)
        one = jnp.ones_like(value)
        keys = [
            jnp.concatenate([jnp.where(keep, key, self.zero), self.key_mark[block]], axis=1)
            for keep in self.keeps
        ]
        values = [
            jnp.concatenate(
                [jnp.where(keep, value, self.zero), jnp.where(keep, one, self.zero)], axis=1
            )
            for keep in self.keeps
        ]
        scores = dot(queries, jnp.concatenate(keys, axis=0), ((1,), (1,)))
        yield
        olds, picked, total = old()
        count = key.shape[0]
        tops, raised, fades = [], [], []
        for head, old in enumerate(olds):
            here = scores[:, head * count : (head + 1) * count]
            top = jnp.maximum(old, jnp.max(here, axis=1, keepdims=True))
            raised.append(jnp.exp2((here - top) * self.scale).astype(jnp.bfloat16))
            fades.append(jnp.exp2((old - top) * self.scale))
            tops.append(top)
        yield
        added = dot(jnp.concatenate(raised, axis=1), jnp.concatenate(values, axis=0))
        fade = jnp.where(self.first, fades[0], fades[1])
        finish(tops, picked * fade + added[:, :LANES], total * fade + added[:, LANES:])


def staggered(tasks):
    running = []
    for task in [*tasks, None, None]:
        running = ([task] if task else []) + running
        running = [one for one in running if next(one, running) is None]


def keep_state(state, pair, rows, tops, picked, total):
    top_ref, picked_ref, total_ref = state
    for head, top in enumerate(tops):
        top_ref[2 * pair + head, rows, :] = jnp.broadcast_to(top, picked.shape)
    picked_ref[pair, rows, :] = picked
    total_ref[pair, rows, :] = total


def read_state(state, pair, rows):
    top_ref, picked_ref, total_ref = state
    tops = [top_ref[2 * pair + head, rows, :] for head in range(2)]
    return tops, picked_ref[pair, rows, :], total_ref[pair, rows, :]


def prepare_kernel(
    owner_ref,
    block_mask_ref,
    segment_ref,
    slot_keys_ref,
    own_ref,
    near_ref,
    project_in_hbm,
    project_out_hbm,
    project_in_ref,
    project_out_ref,
    image_ref,
    query_mark_ref,
    key_mark_ref,
    slot_keys_wide_ref,
    ordered_ref,
    joint_ref,
    places_ref,
    top_ref,
    picked_ref,
    total_ref,
    sems,
    *,
    columns,
    certain,
):
    blk_count = owner_ref.shape[0]
    tok_count = ordered_ref.shape[0]
    rows = own_ref.shape[0]
    copies = [
        pltpu.make_async_copy(project_in_hbm, project_in_ref, sems.at[0]),
        pltpu.make_async_copy(project_out_hbm, project_out_ref, sems.at[1]),
    ]
    for copy in copies:
        copy.start()
    _, own_place = route_of(owner_ref, lax.axis_index("dp"), columns)

    lane = lax.broadcasted_iota(jnp.int32, (1, LANES), 1)
    lane_float = lane.astype(jnp.float32)
    image = segment_ref[...] % blk_count
    image_ref[...] = image
    image = image.astype(jnp.float32)
    image = jnp.transpose(jnp.broadcast_to(image, (LANES, tok_count)))
    image_is = image == lane_float
    for block in range(blk_count):
        at = slice(block * rows, (block + 1) * rows)
        blocked = jnp.zeros((1, LANES), jnp.float32)
        for other in range(blk_count):
            value = jnp.where(block_mask_ref[block, other] == 1, 0.0, NEGATIVE)
            blocked = jnp.where(lane == blk_count + other, value, blocked)
        query_mark_ref[at, :] = jnp.where(image_is[at], NEGATIVE, blocked).astype(jnp.bfloat16)
        block_is = jnp.where(lane == blk_count + block, 1.0, 0.0)
        key_mark_ref[at, :] = jnp.where(
            lane < blk_count, jnp.where(image_is[at], 0.0, 1.0), block_is
        ).astype(jnp.bfloat16)
    wide, experts = slot_keys_wide_ref.shape[0], slot_keys_ref.shape[0]
    column = lax.broadcasted_iota(jnp.int32, (wide, experts), 0)
    expert = lax.broadcasted_iota(jnp.int32, (wide, experts), 1)
    spread = jnp.where(column // blk_count == expert, 1.0, 0.0).astype(jnp.bfloat16)
    slot_keys_wide_ref[...] = dot(spread, slot_keys_ref[...]).astype(jnp.bfloat16)

    copies[0].wait()
    own_index, near_slot = (0, 1) if certain else (own_place, None)
    place_block(own_ref[...].astype(jnp.float32), own_index, project_in_ref, ordered_ref, joint_ref)
    near_place = place_arrived(near_ref, near_slot, project_in_ref, ordered_ref, joint_ref)
    note_place(places_ref, 0, own_place)
    note_place(places_ref, 1, near_place)
    if certain:
        places = (own_place, near_place)
        attention = Attention(
            joint_ref,
            gathered(query_mark_ref, places, rows),
            gathered(key_mark_ref, places, rows),
        )
        state = top_ref, picked_ref, total_ref
        span = slice(0, 2 * rows)
        tasks = []
        for pair in range(ordered_ref.shape[1] // LANES):
            kept = functools.partial(keep_state, state, pair, span)
            tasks.append(attention.begin(kept, pair, 0, 2 * rows, 2 * rows))
        staggered(tasks)
    copies[1].wait()


def middle_kernel(*refs, certain):
    *arrived, project_in_ref, query_mark_ref, key_mark_ref = refs[:-12]
    ordered_ref, joint_ref, places_ref, *state = refs[-6:]
    width = ordered_ref.shape[1]
    for slot, ref in enumerate(arrived, start=2):
        place = place_arrived(
            ref, slot if certain else None, project_in_ref, ordered_ref, joint_ref
        )
        if not certain:
            continue
        rows = ordered_ref.shape[0] // (len(arrived) + 3)
        note_place(places_ref, slot, place)
        places = [read_place(places_ref, n) for n in range(slot)] + [place]
        attention = Attention(
            joint_ref,
            gathered(query_mark_ref, places, rows),
            gathered(key_mark_ref, places, rows),
        )
        stop = slot * rows
        block = slice(stop, stop + rows)
        span = slice(0, stop)
        tasks = []
        for pair in range(width // LANES):
            kept, new = (functools.partial(keep_state, state, pair, at) for at in (span, block))
            old = functools.partial(read_state, state, pair, span)
            tasks.append(attention.extend(kept, pair, stop, block, old))
            tasks.append(attention.begin(new, pair, stop, stop + rows, stop + rows))
        staggered(tasks)


def front_kernel(
    arrived_ref,
    _ordered_ref,
    _joint_ref,
    places_ref,
    top_ref,
    picked_ref,
    total_ref,
    image_ref,
    query_mark_ref,
    key_mark_ref,
    project_in_ref,
    project_out_ref,
    slot_keys_ref,
    expert_in_hbm,
    expert_out_hbm,
    ordered_ref,
    joint_ref,
    hidden_ref,
    slot_in_ref,
    combine_ref,
    expert_in_ref,
    expert_out_ref,
    context_ref,
    moe_normed_ref,
    sems,
    *,
    certain,
):
    tok_count, width = ordered_ref.shape
    blk_count = slot_in_ref.shape[1]
    rows = tok_count // blk_count
    copies = [
        pltpu.make_async_copy(expert_in_hbm, expert_in_ref, sems.at[0]),
        pltpu.make_async_copy(expert_out_hbm, expert_out_ref, sems.at[1]),
    ]
    for copy in copies:
        copy.start()
    last = blk_count - 1
    place = place_arrived(
        arrived_ref, last if certain else None, project_in_ref, ordered_ref, joint_ref
    )
    places = list(range(blk_count))
    if certain:
        places = [read_place(places_ref, n) for n in range(last)] + [place]
    attention = Attention(
        joint_ref,
        gathered(query_mark_ref, places, rows),
        gathered(key_mark_ref, places, rows),
    )
    state = top_ref, picked_ref, total_ref
    stop = last * rows if certain else 0

    def keep_context(pair, rows, tops, picked, total):
        at = slice(pair * LANES, (pair + 1) * LANES)
        context_ref[rows, at] = (picked / total).astype(jnp.bfloat16)

    span, block = slice(0, stop), slice(stop, tok_count)
    tasks = []
    for pair in range(width // LANES):
        kept, new = (functools.partial(keep_context, pair, at) for at in (span, block))
        if certain:
            old = functools.partial(read_state, state, pair, span)
            tasks.append(attention.extend(kept, pair, stop, block, old))
        tasks.append(attention.begin(new, pair, stop, tok_count, tok_count))
    staggered(tasks)

    hidden = (
        ordered_ref[...].astype(jnp.float32) + dot(context_ref[...], project_out_ref[...])
    ).astype(jnp.bfloat16)
    normed = layer_norm(hidden.astype(jnp.float32)).astype(jnp.bfloat16)
    for slot, place in enumerate(places):
        at = slice(slot * rows, (slot + 1) * rows)
        hidden_ref[block_at(place, rows), :] = hidden[at]
        moe_normed_ref[block_at(place, rows), :] = normed[at]
    moe_normed = moe_normed_ref[...]
    logits = dot(slot_keys_ref[...], moe_normed, ((1,), (1,)))
    column_image = lax.broadcasted_iota(jnp.int32, (logits.shape[0], 1), 0) % blk_count
    member = image_ref[...] == column_image
    top = jnp.max(jnp.where(member, logits, NEGATIVE), axis=1, keepdims=True)
    raised = jnp.where(member, jnp.exp(logits - top), 0.0)
    dispatch = raised / jnp.sum(raised, axis=1, keepdims=True)
    slot_in = dot(dispatch.astype(jnp.bfloat16), moe_normed)
    slot_in_ref[...] = slot_in.astype(jnp.bfloat16).reshape(slot_in_ref.shape)
    top = jnp.max(logits, axis=0, keepdims=True)
    raised = jnp.where(member, jnp.exp(logits - top), 0.0)
    combine = raised / jnp.sum(raised, axis=0, keepdims=True)
    combine_ref[...] = jnp.transpose(combine.astype(jnp.bfloat16))
    for copy in copies:
        copy.wait()


def expert_kernel(arrived_ref, expert_in_ref, expert_out_ref, produced_ref, total_ref):
    rows, width = total_ref.shape
    slots = arrived_ref[...].reshape(rows, width)
    hidden_width = expert_in_ref.shape[2]
    step = math.gcd(hidden_width, 768)
    for at in range(0, hidden_width, step):
        inner = dot(slots, expert_in_ref[0, :, at : at + step])
        inner = 0.5 * inner * (1.0 + lax.erf(inner * math.sqrt(0.5)))
        part = dot(inner.astype(jnp.bfloat16), expert_out_ref[0, at : at + step, :])
        total_ref[...] = part if at == 0 else total_ref[...] + part
    produced_ref[...] = total_ref[...].astype(jnp.bfloat16).reshape(produced_ref.shape)


def combine_kernel(hidden_ref, combine_ref, returned_ref, out_hbm, out_ref, sems):
    returned = returned_ref[...].reshape(combine_ref.shape[1], hidden_ref.shape[1])
    count = sems.shape[0]
    rows = hidden_ref.shape[0] // count
    copies = []
    for n in range(count):
        at = slice(n * rows, (n + 1) * rows)
        mixture = dot(combine_ref[at, :], returned)
        out_ref[at, :] = (hidden_ref[at, :].astype(jnp.float32) + mixture).astype(jnp.bfloat16)
        copies.append(pltpu.make_async_copy(out_ref.at[at, :], out_hbm.at[at, :], sems.at[n]))
        copies[-1].start()
    for copy in copies:
        copy.wait()


def resident(*arrays, memory_space=pltpu.VMEM):
    return [pltpu.with_memory_space_constraint(array, memory_space) for array in arrays]


def whole(memory_space=pltpu.VMEM):
    return pl.BlockSpec(memory_space=memory_space)


def per_device(
    patches,
    owner_slot,
    segment_ids,
    block_mask,
    project_in,
    project_out,
    slot_keys,
    expert_in,
    expert_out,
):
    tok_count, width = patches.shape
    blk_count = owner_slot.shape[0]
    rows = tok_count // blk_count
    data_count = lax.axis_size("dp")
    column_count = lax.axis_size("expert")
    expert_count = slot_keys.shape[1]
    columns = expert_count * blk_count
    certain = data_count == blk_count
    params = pltpu.CompilerParams(vmem_limit_bytes=VMEM_LIMIT)

    flips = far_first(data_count)
    tiles = rows * width // (SUBLANES * LANES)
    *sends, own = pl.pallas_call(
        functools.partial(send_kernel, flips=flips, columns=column_count),
        out_shape=[pltpu.VMEM((tiles + 1, SUBLANES, LANES), jnp.bfloat16)] * len(flips)
        + [pltpu.VMEM((rows, width), jnp.bfloat16)],
        in_specs=[whole(pltpu.SMEM), whole()],
        out_specs=[whole()] * (len(flips) + 1),
        compiler_params=params,
        name="send",
    )(*resident(owner_slot, patches, memory_space=pltpu.HBM))
    arrived = []
    for flip, send in zip(flips, sends):
        arrived.append(lax.ppermute(send, "dp", [(i, i ^ flip) for i in range(data_count)]))
    far, near = arrived[:-1], arrived[-1]

    segment = segment_ids.reshape(1, tok_count)
    prepared = pl.pallas_call(
        functools.partial(prepare_kernel, columns=column_count, certain=certain),
        out_shape=[
            pltpu.VMEM(project_in.shape, jnp.bfloat16),
            pltpu.VMEM(project_out.shape, jnp.bfloat16),
            pltpu.VMEM((1, tok_count), jnp.int32),
            pltpu.VMEM((tok_count, LANES), jnp.bfloat16),
            pltpu.VMEM((tok_count, LANES), jnp.bfloat16),
            pltpu.VMEM((columns, width), jnp.bfloat16),
            pltpu.VMEM((tok_count, width), jnp.bfloat16),
            pltpu.VMEM((tok_count, 3 * width), jnp.bfloat16),
            pltpu.VMEM((data_count, LANES), jnp.float32),
            pltpu.VMEM((width // HEAD, tok_count, LANES), jnp.float32),
            pltpu.VMEM((width // LANES, tok_count, LANES), jnp.float32),
            pltpu.VMEM((width // LANES, tok_count, LANES), jnp.float32),
        ],
        in_specs=[whole(pltpu.SMEM)] * 2 + [whole()] * 4 + [whole(pltpu.HBM)] * 2,
        out_specs=[whole()] * 12,
        scratch_shapes=[pltpu.SemaphoreType.DMA((2,))],
        compiler_params=params,
        name="prepare",
    )(
        *resident(owner_slot, block_mask, segment, slot_keys.T, memory_space=pltpu.HBM),
        *resident(own, near),
        *resident(project_in, project_out, memory_space=pltpu.HBM),
    )
    project_in, project_out, image, query_mark, key_mark, slot_keys_wide, *placed = prepared

    placed_shapes = tuple(pltpu.VMEM(array.shape, array.dtype) for array in placed)
    *earlier, last = far
    if earlier:
        base = len(earlier) + 3
        placed = pl.pallas_call(
            functools.partial(middle_kernel, certain=certain),
            out_shape=placed_shapes,
            in_specs=[whole()] * (base + len(placed)),
            out_specs=(whole(),) * len(placed),
            input_output_aliases={base + n: n for n in range(len(placed))},
            compiler_params=params,
            name="middle",
        )(*resident(*earlier, project_in, query_mark, key_mark, *placed))
    *_, hidden, slot_in, combine, expert_in, expert_out = pl.pallas_call(
        functools.partial(front_kernel, certain=certain),
        out_shape=(
            *placed_shapes[:2],
            pltpu.VMEM((tok_count, width), jnp.bfloat16),
            pltpu.VMEM((expert_count, blk_count, width), jnp.bfloat16),
            pltpu.VMEM((tok_count, columns), jnp.bfloat16),
            pltpu.VMEM(expert_in.shape, jnp.bfloat16),
            pltpu.VMEM(expert_out.shape, jnp.bfloat16),
        ),
        in_specs=[whole()] * 13 + [whole(pltpu.HBM)] * 2,
        out_specs=(whole(),) * 7,
        input_output_aliases={1 + n: n for n in range(2)},
        scratch_shapes=[
            pltpu.VMEM((tok_count, width), jnp.bfloat16),
            pltpu.VMEM((tok_count, width), jnp.bfloat16),
            pltpu.SemaphoreType.DMA((2,)),
        ],
        compiler_params=params,
        name="front",
    )(
        *resident(last, *placed, image, query_mark, key_mark),
        *resident(project_in, project_out, slot_keys_wide),
        *resident(expert_in, expert_out, memory_space=pltpu.HBM),
    )
    slots_here = lax.all_to_all(slot_in, AXES, split_axis=0, concat_axis=0, tiled=True)
    produced = pl.pallas_call(
        expert_kernel,
        out_shape=pltpu.VMEM(slots_here.shape, jnp.bfloat16),
        in_specs=[whole()] * 3,
        out_specs=whole(),
        scratch_shapes=[pltpu.VMEM((columns, width), jnp.float32)],
        compiler_params=params,
        name="expert",
    )(*resident(slots_here, expert_in, expert_out))
    returned = lax.all_to_all(produced, AXES, split_axis=0, concat_axis=0, tiled=True)
    return pl.pallas_call(
        combine_kernel,
        out_shape=jax.ShapeDtypeStruct((tok_count, width), jnp.bfloat16),
        in_specs=[whole()] * 3,
        out_specs=whole(pltpu.HBM),
        scratch_shapes=[
            pltpu.VMEM((tok_count, width), jnp.bfloat16),
            pltpu.SemaphoreType.DMA((blk_count,)),
        ],
        compiler_params=params,
        name="combine",
    )(*resident(hidden, combine, returned))


def solution(mesh):
    in_specs = (
        P(AXES, None),
        P(AXES),
        P(AXES),
        P(AXES, None),
        P(),
        P(),
        P(),
        P(AXES, None, None),
        P(AXES, None, None),
    )
    return jax.shard_map(
        per_device,
        mesh=mesh,
        in_specs=in_specs,
        out_specs=P(AXES, None),
        check_vma=False,
    )
```

```python
import functools
import math

import jax
import jax.numpy as jnp
from jax import lax
from jax.experimental import pallas as pl
from jax.experimental.pallas import tpu as pltpu
from jax.sharding import PartitionSpec as P


HEAD = 64
LANES = 128
SUBLANES = 8
EPS = 1e-06
NEGATIVE = -1e30
AXES = ("dp", "expert")
VMEM_LIMIT = 24 << 20


def layer_norm(values):
    centred = values - jnp.mean(values, axis=-1, keepdims=True)
    variance = jnp.mean(centred * centred, axis=-1, keepdims=True)
    return centred * lax.rsqrt(variance + EPS)


def dot(a, b, dims=((1,), (0,))):
    return lax.dot_general(a, b, (dims, ((), ())), preferred_element_type=jnp.float32)


def far_first(count):
    return [*range(2, count), 1]


def route_of(owner_ref, target, columns):
    blk_count = owner_ref.shape[0]
    source = jnp.int32(0)
    place = jnp.int32(-1)
    for block in range(blk_count):
        owner = owner_ref[block]
        hit = owner // (blk_count * columns) == target
        source = jnp.where(hit, block, source)
        place = jnp.where(hit, owner % blk_count, place)
    return source, place


def packed(block):
    rows, width = block.shape
    tiles = [
        block[:, at : at + LANES].reshape(rows // SUBLANES, SUBLANES, LANES)
        for at in range(0, width, LANES)
    ]
    return jnp.concatenate(tiles, axis=0).astype(jnp.bfloat16)


def unpacked(tiles, width):
    count = tiles.shape[0] * LANES // width
    parts = [
        tiles[at : at + count].reshape(count * SUBLANES, LANES)
        for at in range(0, tiles.shape[0], count)
    ]
    return jnp.concatenate(parts, axis=1)


def send_kernel(owner_ref, patches_ref, *refs, flips, columns):
    sends, own_ref = refs[:-1], refs[-1]
    rows = own_ref.shape[0]
    me = lax.axis_index("dp")

    def chosen(flip):
        source, place = route_of(owner_ref, me ^ flip, columns)
        return patches_ref[pl.ds(pl.multiple_of(source * rows, rows), rows), :], place

    for flip, send in zip(flips, sends):
        block, place = chosen(flip)
        tiles = send.shape[0] - 1
        send[:tiles] = packed(block.astype(jnp.float32))
        tag = jnp.full((1, SUBLANES, LANES), place.astype(jnp.float32))
        send[tiles : tiles + 1] = tag.astype(jnp.bfloat16)
    own_ref[...] = chosen(0)[0]


def block_at(index, rows):
    if isinstance(index, int):
        return slice(index * rows, (index + 1) * rows)
    return pl.ds(pl.multiple_of(index * rows, rows), rows)


def place_block(block, index, project_in_ref, ordered_ref, joint_ref):
    at = block_at(index, block.shape[0])
    ordered_ref[at, :] = block.astype(jnp.bfloat16)
    normed = layer_norm(block).astype(jnp.bfloat16)
    joint_ref[at, :] = dot(normed, project_in_ref[...]).astype(jnp.bfloat16)


def place_arrived(ref, slot, project_in_ref, ordered_ref, joint_ref):
    tiles = ref.shape[0] - 1
    place = jnp.max(ref[tiles].astype(jnp.float32)).astype(jnp.int32)

    def fill(index):
        block = unpacked(ref[:tiles].astype(jnp.float32), ordered_ref.shape[1])
        place_block(block, index, project_in_ref, ordered_ref, joint_ref)

    if slot is not None:
        fill(slot)
    else:
        pl.when(place >= 0)(lambda: fill(place))
    return place


def read_place(places_ref, slot):
    return jnp.max(places_ref[slot : slot + 1, :]).astype(jnp.int32)


def note_place(places_ref, slot, place):
    places_ref[slot : slot + 1, :] = jnp.full((1, LANES), place.astype(jnp.float32))


def gathered(mark_ref, places, rows):
    return jnp.concatenate([mark_ref[block_at(place, rows), :] for place in places], axis=0)


class Attention:
    def __init__(self, joint_ref, query_mark, key_mark):
        self.joint_ref, self.query_mark, self.key_mark = joint_ref, query_mark, key_mark
        self.width = joint_ref.shape[1] // 3
        self.scale = HEAD ** (-0.5) * math.log2(math.e)
        first = lax.broadcasted_iota(jnp.int32, (1, LANES), 1) < HEAD
        self.first, self.keeps = first, (first, ~first)
        self.zero = jnp.zeros((), jnp.bfloat16)

    def part(self, which, pair, rows):
        at = which * self.width + pair * LANES
        return self.joint_ref[rows, at : at + LANES]

    def begin(self, finish, pair, start, stop, keys_stop):
        query = self.part(0, pair, slice(start, stop))
        span = slice(0, keys_stop)
        keys = jnp.concatenate([self.part(1, pair, span), self.key_mark[span]], axis=1)
        ones = jnp.ones((keys_stop, LANES), jnp.bfloat16)
        values = jnp.concatenate([self.part(2, pair, span), ones], axis=1)
        scores = []
        for keep in self.keeps:
            queries = jnp.concatenate(
                [jnp.where(keep, query, self.zero), self.query_mark[start:stop]], axis=1
            )
            scores.append(dot(queries, keys, ((1,), (1,))))
        yield
        tops = [jnp.max(part, axis=1, keepdims=True) for part in scores]
        raised = [
            jnp.exp2((part - top) * self.scale).astype(jnp.bfloat16)
            for part, top in zip(scores, tops)
        ]
        yield
        parts = [dot(part, values) for part in raised]
        picked = jnp.where(self.first, parts[0][:, :LANES], parts[1][:, :LANES])
        total = jnp.where(self.first, parts[0][:, LANES:], parts[1][:, LANES:])
        finish(tops, picked, total)

    def extend(self, finish, pair, stop, block, old):
        queries = jnp.concatenate(
            [self.part(0, pair, slice(0, stop)), self.query_mark[:stop]], axis=1
        )
        key, value = self.part(1, pair, block), self.part(2, pair, block)
        one = jnp.ones_like(value)
        keys = [
            jnp.concatenate([jnp.where(keep, key, self.zero), self.key_mark[block]], axis=1)
            for keep in self.keeps
        ]
        values = [
            jnp.concatenate(
                [jnp.where(keep, value, self.zero), jnp.where(keep, one, self.zero)], axis=1
            )
            for keep in self.keeps
        ]
        scores = dot(queries, jnp.concatenate(keys, axis=0), ((1,), (1,)))
        yield
        olds, picked, total = old()
        count = key.shape[0]
        tops, raised, fades = [], [], []
        for head, old in enumerate(olds):
            here = scores[:, head * count : (head + 1) * count]
            top = jnp.maximum(old, jnp.max(here, axis=1, keepdims=True))
            raised.append(jnp.exp2((here - top) * self.scale).astype(jnp.bfloat16))
            fades.append(jnp.exp2((old - top) * self.scale))
            tops.append(top)
        yield
        added = dot(jnp.concatenate(raised, axis=1), jnp.concatenate(values, axis=0))
        fade = jnp.where(self.first, fades[0], fades[1])
        finish(tops, picked * fade + added[:, :LANES], total * fade + added[:, LANES:])


def staggered(tasks):
    tasks, running = list(tasks), []
    while tasks or running:
        task = tasks.pop(0) if tasks else None
        running = ([task] if task else []) + running
        running = [one for one in running if next(one, running) is None]


def keep_state(state, pair, rows, tops, picked, total):
    top_ref, picked_ref, total_ref = state
    for head, top in enumerate(tops):
        top_ref[2 * pair + head, rows, :] = jnp.broadcast_to(top, picked.shape)
    picked_ref[pair, rows, :] = picked
    total_ref[pair, rows, :] = total


def read_state(state, pair, rows):
    top_ref, picked_ref, total_ref = state
    tops = [top_ref[2 * pair + head, rows, :] for head in range(2)]
    return tops, picked_ref[pair, rows, :], total_ref[pair, rows, :]


def prepare_kernel(
    owner_hbm,
    block_mask_hbm,
    segment_hbm,
    slot_keys_hbm,
    own_ref,
    project_in_hbm,
    project_in_ref,
    image_ref,
    query_mark_ref,
    key_mark_ref,
    slot_keys_wide_ref,
    ordered_ref,
    joint_ref,
    places_ref,
    owner_ref,
    block_mask_ref,
    segment_ref,
    slot_keys_ref,
    small_sems,
    sems,
    *,
    columns,
    certain,
):
    blk_count = owner_ref.shape[0]
    tok_count = ordered_ref.shape[0]
    rows = own_ref.shape[0]
    small = (
        (owner_hbm, owner_ref),
        (block_mask_hbm, block_mask_ref),
        (segment_hbm, segment_ref),
        (slot_keys_hbm, slot_keys_ref),
    )
    small_copies = [
        pltpu.make_async_copy(source, target, small_sems.at[n])
        for n, (source, target) in enumerate(small)
    ]
    width = ordered_ref.shape[1]
    pieces = sems.shape[1]
    span = width // pieces
    bands = [slice(which * width, (which + 1) * width) for which in range(3)]
    blocks = [slice(piece * span, (piece + 1) * span) for piece in range(pieces)]
    copies = [
        [
            pltpu.make_async_copy(
                project_in_hbm.at[at, band], project_in_ref.at[at, band], sems.at[n, piece]
            )
            for piece, at in enumerate(blocks)
        ]
        for n, band in enumerate(bands)
    ]
    for copy in small_copies + sum(copies, []):
        copy.start()
    for copy in small_copies:
        copy.wait()
    _, own_place = route_of(owner_ref, lax.axis_index("dp"), columns)

    lane = lax.broadcasted_iota(jnp.int32, (1, LANES), 1)
    lane_float = lane.astype(jnp.float32)
    image = segment_ref[...] % blk_count
    image_ref[...] = image
    image = image.astype(jnp.float32)
    image = jnp.transpose(jnp.broadcast_to(image, (LANES, tok_count)))
    image_is = image == lane_float
    for block in range(blk_count):
        at = slice(block * rows, (block + 1) * rows)
        blocked = jnp.zeros((1, LANES), jnp.float32)
        for other in range(blk_count):
            value = jnp.where(block_mask_ref[block, other] == 1, 0.0, NEGATIVE)
            blocked = jnp.where(lane == blk_count + other, value, blocked)
        query_mark_ref[at, :] = jnp.where(image_is[at], NEGATIVE, blocked).astype(jnp.bfloat16)
        block_is = jnp.where(lane == blk_count + block, 1.0, 0.0)
        key_mark_ref[at, :] = jnp.where(
            lane < blk_count, jnp.where(image_is[at], 0.0, 1.0), block_is
        ).astype(jnp.bfloat16)
    wide, experts = slot_keys_wide_ref.shape[0], slot_keys_ref.shape[0]
    column = lax.broadcasted_iota(jnp.int32, (wide, experts), 0)
    expert = lax.broadcasted_iota(jnp.int32, (wide, experts), 1)
    spread = jnp.where(column // blk_count == expert, 1.0, 0.0).astype(jnp.bfloat16)
    slot_keys_wide_ref[...] = dot(spread, slot_keys_ref[...]).astype(jnp.bfloat16)

    at = block_at(0 if certain else own_place, rows)
    block = own_ref[...]
    ordered_ref[at, :] = block
    normed = layer_norm(block.astype(jnp.float32)).astype(jnp.bfloat16)
    for n, band in enumerate(bands):
        for copy in copies[n]:
            copy.wait()
        joint_ref[at, band] = dot(normed, project_in_ref[:, band]).astype(jnp.bfloat16)
    note_place(places_ref, 0, own_place)


def near_kernel(
    near_ref,
    project_in_ref,
    query_mark_ref,
    key_mark_ref,
    _ordered_ref,
    _joint_ref,
    _places_ref,
    ordered_ref,
    joint_ref,
    places_ref,
    *state,
    rows,
    certain,
):
    place = place_arrived(
        near_ref, 1 if certain else None, project_in_ref, ordered_ref, joint_ref
    )
    if certain:
        note_place(places_ref, 1, place)
        places = read_place(places_ref, 0), place
        begin_near(places, joint_ref, query_mark_ref, key_mark_ref, state, rows)


def begin_near(places, joint_ref, query_mark_ref, key_mark_ref, state, rows):
    attention = Attention(
        joint_ref,
        gathered(query_mark_ref, places, rows),
        gathered(key_mark_ref, places, rows),
    )
    span = slice(0, 2 * rows)
    tasks = []
    for pair in range(attention.width // LANES):
        kept = functools.partial(keep_state, state, pair, span)
        tasks.append(attention.begin(kept, pair, 0, 2 * rows, 2 * rows))
    staggered(tasks)


def middle_kernel(*refs, certain):
    *arrived, project_in_ref, query_mark_ref, key_mark_ref = refs[:-15]
    project_out_hbm, ordered_ref, joint_ref, places_ref, *state = refs[-9:-2]
    project_out_ref, sems = refs[-2:]
    pieces = sems.shape[0]
    span = project_out_ref.shape[0] // pieces
    copies = []
    for piece in range(pieces):
        at = slice(piece * span, (piece + 1) * span)
        copies.append(
            pltpu.make_async_copy(
                project_out_hbm.at[at, :], project_out_ref.at[at, :], sems.at[piece]
            )
        )
        copies[-1].start()
    width = ordered_ref.shape[1]
    for slot, ref in enumerate(arrived, start=2):
        place = place_arrived(
            ref, slot if certain else None, project_in_ref, ordered_ref, joint_ref
        )
        if not certain:
            continue
        rows = ordered_ref.shape[0] // (len(arrived) + 3)
        note_place(places_ref, slot, place)
        places = [read_place(places_ref, n) for n in range(slot)] + [place]
        attention = Attention(
            joint_ref,
            gathered(query_mark_ref, places, rows),
            gathered(key_mark_ref, places, rows),
        )
        stop = slot * rows
        block = slice(stop, stop + rows)
        span = slice(0, stop)
        tasks = []
        for pair in range(width // LANES):
            kept, new = (functools.partial(keep_state, state, pair, at) for at in (span, block))
            old = functools.partial(read_state, state, pair, span)
            tasks.append(attention.extend(kept, pair, stop, block, old))
            tasks.append(attention.begin(new, pair, stop, stop + rows, stop + rows))
        staggered(tasks)
    for copy in copies:
        copy.wait()


def front_kernel(
    arrived_ref,
    _ordered_ref,
    _joint_ref,
    places_ref,
    top_ref,
    picked_ref,
    total_ref,
    image_ref,
    query_mark_ref,
    key_mark_ref,
    project_in_ref,
    project_out_ref,
    slot_keys_ref,
    ordered_ref,
    joint_ref,
    hidden_ref,
    slot_in_ref,
    combine_ref,
    context_ref,
    moe_normed_ref,
    logits_ref,
    *,
    certain,
):
    tok_count, width = ordered_ref.shape
    blk_count = slot_in_ref.shape[1]
    rows = tok_count // blk_count
    last = blk_count - 1
    place = place_arrived(
        arrived_ref, last if certain else None, project_in_ref, ordered_ref, joint_ref
    )
    places = list(range(blk_count))
    if certain:
        places = [read_place(places_ref, n) for n in range(last)] + [place]
    attention = Attention(
        joint_ref,
        gathered(query_mark_ref, places, rows),
        gathered(key_mark_ref, places, rows),
    )
    state = top_ref, picked_ref, total_ref
    stop = last * rows if certain else 0

    def keep_context(pair, rows, tops, picked, total):
        at = slice(pair * LANES, (pair + 1) * LANES)
        context_ref[rows, at] = (picked / total).astype(jnp.bfloat16)

    column_image = lax.broadcasted_iota(jnp.int32, (logits_ref.shape[0], 1), 0) % blk_count

    def settle(slot, place):
        at, out = block_at(slot, rows), block_at(place, rows)
        projected = dot(context_ref[at, :], project_out_ref[...])
        yield
        hidden = (ordered_ref[at, :].astype(jnp.float32) + projected).astype(jnp.bfloat16)
        hidden_ref[out, :] = hidden
        moe_normed = layer_norm(hidden.astype(jnp.float32)).astype(jnp.bfloat16)
        moe_normed_ref[out, :] = moe_normed
        yield
        logits = dot(slot_keys_ref[...], moe_normed, ((1,), (1,)))
        logits_ref[:, out] = logits
        yield
        top = jnp.max(logits, axis=0, keepdims=True)
        member = image_ref[:, out] == column_image
        raised = jnp.where(member, jnp.exp(logits - top), 0.0)
        combine = raised / jnp.sum(raised, axis=0, keepdims=True)
        combine_ref[out, :] = jnp.transpose(combine.astype(jnp.bfloat16))

    span, block = slice(0, stop), slice(stop, tok_count)
    pairs = range(width // LANES)
    grown = [
        attention.extend(
            functools.partial(keep_context, pair, span),
            pair,
            stop,
            block,
            functools.partial(read_state, state, pair, span),
        )
        for pair in pairs
        if certain
    ]
    fresh = [
        attention.begin(functools.partial(keep_context, pair, block), pair, stop, tok_count, tok_count)
        for pair in pairs
    ]
    settled = [settle(slot, place) for slot, place in enumerate(places)]
    if certain:
        staggered(
            [*(task for both in zip(grown, fresh) for task in both), None, None, *settled]
        )
    else:
        staggered([*fresh, None, None, *settled])

    moe_normed = moe_normed_ref[...]
    logits = logits_ref[...]
    member = image_ref[...] == column_image
    top = jnp.max(jnp.where(member, logits, NEGATIVE), axis=1, keepdims=True)
    raised = jnp.where(member, jnp.exp(logits - top), 0.0)
    dispatch = raised / jnp.sum(raised, axis=1, keepdims=True)
    slot_in = dot(dispatch.astype(jnp.bfloat16), moe_normed)
    slot_in_ref[...] = slot_in.astype(jnp.bfloat16).reshape(slot_in_ref.shape)


def expert_kernel(arrived_ref, expert_in_ref, expert_out_ref, produced_ref, total_ref):
    rows, width = total_ref.shape
    slots = arrived_ref[...].reshape(rows, width)
    hidden_width = expert_in_ref.shape[2]
    step = math.gcd(hidden_width, 768)
    for at in range(0, hidden_width, step):
        inner = dot(slots, expert_in_ref[0, :, at : at + step])
        inner = 0.5 * inner * (1.0 + lax.erf(inner * math.sqrt(0.5)))
        part = dot(inner.astype(jnp.bfloat16), expert_out_ref[0, at : at + step, :])
        total_ref[...] = part if at == 0 else total_ref[...] + part
    produced_ref[...] = total_ref[...].astype(jnp.bfloat16).reshape(produced_ref.shape)


def combine_kernel(hidden_ref, combine_ref, returned_ref, out_hbm, out_ref, sems):
    returned = returned_ref[...].reshape(combine_ref.shape[1], hidden_ref.shape[1])
    count = sems.shape[0]
    rows = hidden_ref.shape[0] // count
    copies = []
    for n in range(count):
        at = slice(n * rows, (n + 1) * rows)
        mixture = dot(combine_ref[at, :], returned)
        out_ref[at, :] = (hidden_ref[at, :].astype(jnp.float32) + mixture).astype(jnp.bfloat16)
        copies.append(pltpu.make_async_copy(out_ref.at[at, :], out_hbm.at[at, :], sems.at[n]))
        copies[-1].start()
    for copy in copies:
        copy.wait()


def resident(*arrays, memory_space=pltpu.VMEM):
    return [pltpu.with_memory_space_constraint(array, memory_space) for array in arrays]


def whole(memory_space=pltpu.VMEM):
    return pl.BlockSpec(memory_space=memory_space)


def per_device(
    patches,
    owner_slot,
    segment_ids,
    block_mask,
    project_in,
    project_out,
    slot_keys,
    expert_in,
    expert_out,
):
    tok_count, width = patches.shape
    blk_count = owner_slot.shape[0]
    rows = tok_count // blk_count
    data_count = lax.axis_size("dp")
    column_count = lax.axis_size("expert")
    expert_count = slot_keys.shape[1]
    columns = expert_count * blk_count
    certain = data_count == blk_count
    params = pltpu.CompilerParams(vmem_limit_bytes=VMEM_LIMIT)

    flips = far_first(data_count)
    tiles = rows * width // (SUBLANES * LANES)
    *sends, own = pl.pallas_call(
        functools.partial(send_kernel, flips=flips, columns=column_count),
        out_shape=[pltpu.VMEM((tiles + 1, SUBLANES, LANES), jnp.bfloat16)] * len(flips)
        + [pltpu.VMEM((rows, width), jnp.bfloat16)],
        in_specs=[whole(pltpu.SMEM), whole()],
        out_specs=[whole()] * (len(flips) + 1),
        compiler_params=params,
        name="send",
    )(*resident(owner_slot, patches, memory_space=pltpu.HBM))
    arrived = []
    for flip, send in zip(flips, sends):
        arrived.append(lax.ppermute(send, "dp", [(i, i ^ flip) for i in range(data_count)]))
    far, near = arrived[:-1], arrived[-1]

    segment = segment_ids.reshape(1, tok_count)
    prepared = pl.pallas_call(
        functools.partial(prepare_kernel, columns=column_count, certain=certain),
        out_shape=[
            pltpu.VMEM(project_in.shape, jnp.bfloat16),
            pltpu.VMEM((1, tok_count), jnp.int32),
            pltpu.VMEM((tok_count, LANES), jnp.bfloat16),
            pltpu.VMEM((tok_count, LANES), jnp.bfloat16),
            pltpu.VMEM((columns, width), jnp.bfloat16),
            pltpu.VMEM((tok_count, width), jnp.bfloat16),
            pltpu.VMEM((tok_count, 3 * width), jnp.bfloat16),
            pltpu.VMEM((data_count, LANES), jnp.float32),
        ],
        in_specs=[whole(pltpu.HBM)] * 4 + [whole(), whole(pltpu.HBM)],
        out_specs=[whole()] * 8,
        scratch_shapes=[
            pltpu.SMEM(owner_slot.shape, jnp.int32),
            pltpu.SMEM(block_mask.shape, jnp.int32),
            pltpu.VMEM(segment.shape, jnp.int32),
            pltpu.VMEM(slot_keys.shape[::-1], jnp.bfloat16),
            pltpu.SemaphoreType.DMA((4,)),
            pltpu.SemaphoreType.DMA((3, width // (2 * LANES))),
        ],
        compiler_params=params,
        name="prepare",
    )(
        *resident(owner_slot, block_mask, segment, slot_keys.T, memory_space=pltpu.HBM),
        *resident(own),
        *resident(project_in, memory_space=pltpu.HBM),
    )
    project_in, image, query_mark, key_mark, slot_keys_wide, *placed = prepared
    placed = pl.pallas_call(
        functools.partial(near_kernel, rows=rows, certain=certain),
        out_shape=[
            *(pltpu.VMEM(array.shape, array.dtype) for array in placed),
            pltpu.VMEM((width // HEAD, tok_count, LANES), jnp.float32),
            pltpu.VMEM((width // LANES, tok_count, LANES), jnp.float32),
            pltpu.VMEM((width // LANES, tok_count, LANES), jnp.float32),
        ],
        in_specs=[whole()] * 7,
        out_specs=[whole()] * 6,
        input_output_aliases={4 + n: n for n in range(3)},
        compiler_params=params,
        name="near",
    )(*resident(near, project_in, query_mark, key_mark, *placed))

    placed_shapes = tuple(pltpu.VMEM(array.shape, array.dtype) for array in placed)
    *earlier, last = far
    base = len(earlier) + 3
    *placed, project_out = pl.pallas_call(
        functools.partial(middle_kernel, certain=certain),
        out_shape=(*placed_shapes, pltpu.VMEM(project_out.shape, jnp.bfloat16)),
        in_specs=[whole()] * (base + len(placed)) + [whole(pltpu.HBM)],
        out_specs=(whole(),) * (len(placed) + 1),
        input_output_aliases={base + n: n for n in range(len(placed))},
        scratch_shapes=[pltpu.SemaphoreType.DMA((width // (2 * LANES),))],
        compiler_params=params,
        name="middle",
    )(
        *resident(*earlier, project_in, query_mark, key_mark, *placed),
        *resident(project_out, memory_space=pltpu.HBM),
    )
    *_, hidden, slot_in, combine = pl.pallas_call(
        functools.partial(front_kernel, certain=certain),
        out_shape=(
            *placed_shapes[:2],
            pltpu.VMEM((tok_count, width), jnp.bfloat16),
            pltpu.VMEM((expert_count, blk_count, width), jnp.bfloat16),
            pltpu.VMEM((tok_count, columns), jnp.bfloat16),
        ),
        in_specs=[whole()] * 13,
        out_specs=(whole(),) * 5,
        input_output_aliases={1 + n: n for n in range(2)},
        scratch_shapes=[pltpu.VMEM((tok_count, width), jnp.bfloat16)] * 2
        + [pltpu.VMEM((columns, tok_count), jnp.float32)],
        compiler_params=params,
        name="front",
    )(
        *resident(last, *placed, image, query_mark, key_mark),
        *resident(project_in, project_out, slot_keys_wide),
    )
    slots_here = lax.all_to_all(slot_in, AXES, split_axis=0, concat_axis=0, tiled=True)
    produced = pl.pallas_call(
        expert_kernel,
        out_shape=pltpu.VMEM(slots_here.shape, jnp.bfloat16),
        in_specs=[whole()] * 3,
        out_specs=whole(),
        scratch_shapes=[pltpu.VMEM((columns, width), jnp.float32)],
        compiler_params=params,
        name="expert",
    )(*resident(slots_here, expert_in, expert_out))
    returned = lax.all_to_all(produced, AXES, split_axis=0, concat_axis=0, tiled=True)
    return pl.pallas_call(
        combine_kernel,
        out_shape=jax.ShapeDtypeStruct((tok_count, width), jnp.bfloat16),
        in_specs=[whole()] * 3,
        out_specs=whole(pltpu.HBM),
        scratch_shapes=[
            pltpu.VMEM((tok_count, width), jnp.bfloat16),
            pltpu.SemaphoreType.DMA((blk_count,)),
        ],
        compiler_params=params,
        name="combine",
    )(*resident(hidden, combine, returned))


def solution(mesh):
    in_specs = (
        P(AXES, None),
        P(AXES),
        P(AXES),
        P(AXES, None),
        P(),
        P(),
        P(),
        P(AXES, None, None),
        P(AXES, None, None),
    )
    return jax.shard_map(
        per_device,
        mesh=mesh,
        in_specs=in_specs,
        out_specs=P(AXES, None),
        check_vma=False,
    )
```

```python
import functools
import math

import jax
import jax.numpy as jnp
from jax import lax
from jax.experimental import pallas as pl
from jax.experimental.pallas import tpu as pltpu
from jax.sharding import PartitionSpec as P


HEAD = 64
LANES = 128
SUBLANES = 8
EPS = 1e-06
NEGATIVE = -1e30
AXES = ("dp", "expert")
VMEM_LIMIT = 24 << 20


def layer_norm(values):
    centred = values - jnp.mean(values, axis=-1, keepdims=True)
    variance = jnp.mean(centred * centred, axis=-1, keepdims=True)
    return centred * lax.rsqrt(variance + EPS)


def dot(a, b, dims=((1,), (0,))):
    return lax.dot_general(a, b, (dims, ((), ())), preferred_element_type=jnp.float32)


def far_first(count):
    return [*range(2, count), 1]


def route_of(owner_ref, target, columns):
    blk_count = owner_ref.shape[0]
    source = jnp.int32(0)
    place = jnp.int32(-1)
    for block in range(blk_count):
        owner = owner_ref[block]
        hit = owner // (blk_count * columns) == target
        source = jnp.where(hit, block, source)
        place = jnp.where(hit, owner % blk_count, place)
    return source, place


def packed(block):
    rows, width = block.shape
    tiles = [
        block[:, at : at + LANES].reshape(rows // SUBLANES, SUBLANES, LANES)
        for at in range(0, width, LANES)
    ]
    return jnp.concatenate(tiles, axis=0).astype(jnp.bfloat16)


def unpacked(tiles, width):
    count = tiles.shape[0] * LANES // width
    parts = [
        tiles[at : at + count].reshape(count * SUBLANES, LANES)
        for at in range(0, tiles.shape[0], count)
    ]
    return jnp.concatenate(parts, axis=1)


def send_kernel(owner_ref, patches_ref, *refs, flips, columns):
    sends, own_ref = refs[:-1], refs[-1]
    rows = own_ref.shape[0]
    me = lax.axis_index("dp")

    def chosen(flip):
        source, place = route_of(owner_ref, me ^ flip, columns)
        return patches_ref[pl.ds(pl.multiple_of(source * rows, rows), rows), :], place

    for flip, send in zip(flips, sends):
        block, place = chosen(flip)
        tiles = send.shape[0] - 1
        send[:tiles] = packed(block.astype(jnp.float32))
        tag = jnp.full((1, SUBLANES, LANES), place.astype(jnp.float32))
        send[tiles : tiles + 1] = tag.astype(jnp.bfloat16)
    own_ref[...] = chosen(0)[0]


def block_at(index, rows):
    if isinstance(index, int):
        return slice(index * rows, (index + 1) * rows)
    return pl.ds(pl.multiple_of(index * rows, rows), rows)


def place_block(block, index, project_in_ref, ordered_ref, joint_ref):
    at = block_at(index, block.shape[0])
    ordered_ref[at, :] = block.astype(jnp.bfloat16)
    normed = layer_norm(block).astype(jnp.bfloat16)
    joint_ref[at, :] = dot(normed, project_in_ref[...]).astype(jnp.bfloat16)


def place_arrived(ref, slot, project_in_ref, ordered_ref, joint_ref):
    tiles = ref.shape[0] - 1
    place = jnp.max(ref[tiles].astype(jnp.float32)).astype(jnp.int32)

    def fill(index):
        block = unpacked(ref[:tiles].astype(jnp.float32), ordered_ref.shape[1])
        place_block(block, index, project_in_ref, ordered_ref, joint_ref)

    if slot is not None:
        fill(slot)
    else:
        pl.when(place >= 0)(lambda: fill(place))
    return place


def read_place(places_ref, slot):
    return jnp.max(places_ref[slot : slot + 1, :]).astype(jnp.int32)


def note_place(places_ref, slot, place):
    places_ref[slot : slot + 1, :] = jnp.full((1, LANES), place.astype(jnp.float32))


def gathered(mark_ref, places, rows):
    return jnp.concatenate([mark_ref[block_at(place, rows), :] for place in places], axis=0)


class Attention:
    def __init__(self, joint_ref, query_mark, key_mark):
        self.joint_ref, self.query_mark, self.key_mark = joint_ref, query_mark, key_mark
        self.width = joint_ref.shape[1] // 3
        self.scale = HEAD ** (-0.5) * math.log2(math.e)
        first = lax.broadcasted_iota(jnp.int32, (1, LANES), 1) < HEAD
        self.first, self.keeps = first, (first, ~first)
        self.zero = jnp.zeros((), jnp.bfloat16)

    def part(self, which, pair, rows):
        at = which * self.width + pair * LANES
        return self.joint_ref[rows, at : at + LANES]

    def begin(self, finish, pair, start, stop, keys_stop):
        query = self.part(0, pair, slice(start, stop))
        span = slice(0, keys_stop)
        keys = jnp.concatenate([self.part(1, pair, span), self.key_mark[span]], axis=1)
        ones = jnp.ones((keys_stop, LANES), jnp.bfloat16)
        values = jnp.concatenate([self.part(2, pair, span), ones], axis=1)
        scores = []
        for keep in self.keeps:
            queries = jnp.concatenate(
                [jnp.where(keep, query, self.zero), self.query_mark[start:stop]], axis=1
            )
            scores.append(dot(queries, keys, ((1,), (1,))))
        yield
        tops = [jnp.max(part, axis=1, keepdims=True) for part in scores]
        raised = [
            jnp.exp2((part - top) * self.scale).astype(jnp.bfloat16)
            for part, top in zip(scores, tops)
        ]
        yield
        parts = [dot(part, values) for part in raised]
        picked = jnp.where(self.first, parts[0][:, :LANES], parts[1][:, :LANES])
        total = jnp.where(self.first, parts[0][:, LANES:], parts[1][:, LANES:])
        finish(tops, picked, total)

    def extend(self, finish, pair, stop, block, old):
        queries = jnp.concatenate(
            [self.part(0, pair, slice(0, stop)), self.query_mark[:stop]], axis=1
        )
        key, value = self.part(1, pair, block), self.part(2, pair, block)
        one = jnp.ones_like(value)
        keys = [
            jnp.concatenate([jnp.where(keep, key, self.zero), self.key_mark[block]], axis=1)
            for keep in self.keeps
        ]
        values = [
            jnp.concatenate(
                [jnp.where(keep, value, self.zero), jnp.where(keep, one, self.zero)], axis=1
            )
            for keep in self.keeps
        ]
        scores = dot(queries, jnp.concatenate(keys, axis=0), ((1,), (1,)))
        yield
        olds, picked, total = old()
        count = key.shape[0]
        tops, raised, fades = [], [], []
        for head, old in enumerate(olds):
            here = scores[:, head * count : (head + 1) * count]
            top = jnp.maximum(old, jnp.max(here, axis=1, keepdims=True))
            raised.append(jnp.exp2((here - top) * self.scale).astype(jnp.bfloat16))
            fades.append(jnp.exp2((old - top) * self.scale))
            tops.append(top)
        yield
        added = dot(jnp.concatenate(raised, axis=1), jnp.concatenate(values, axis=0))
        fade = jnp.where(self.first, fades[0], fades[1])
        finish(tops, picked * fade + added[:, :LANES], total * fade + added[:, LANES:])


def staggered(tasks):
    tasks, running = list(tasks), []
    while tasks or running:
        task = tasks.pop(0) if tasks else None
        running = ([task] if task else []) + running
        running = [one for one in running if next(one, running) is None]


def keep_state(state, pair, rows, tops, picked, total):
    top_ref, picked_ref, total_ref = state
    for head, top in enumerate(tops):
        top_ref[2 * pair + head, rows, :] = jnp.broadcast_to(top, picked.shape)
    picked_ref[pair, rows, :] = picked
    total_ref[pair, rows, :] = total


def read_state(state, pair, rows):
    top_ref, picked_ref, total_ref = state
    tops = [top_ref[2 * pair + head, rows, :] for head in range(2)]
    return tops, picked_ref[pair, rows, :], total_ref[pair, rows, :]


def prepare_kernel(
    owner_hbm,
    block_mask_hbm,
    segment_hbm,
    slot_keys_hbm,
    own_ref,
    project_in_hbm,
    project_out_hbm,
    project_in_ref,
    project_out_ref,
    image_ref,
    query_mark_ref,
    key_mark_ref,
    slot_keys_wide_ref,
    ordered_ref,
    joint_ref,
    places_ref,
    owner_ref,
    block_mask_ref,
    segment_ref,
    slot_keys_ref,
    small_sems,
    sems,
    *,
    columns,
    certain,
):
    blk_count = owner_ref.shape[0]
    tok_count = ordered_ref.shape[0]
    rows = own_ref.shape[0]
    small = (
        (owner_hbm, owner_ref),
        (block_mask_hbm, block_mask_ref),
        (segment_hbm, segment_ref),
        (slot_keys_hbm, slot_keys_ref),
    )
    small_copies = [
        pltpu.make_async_copy(source, target, small_sems.at[n])
        for n, (source, target) in enumerate(small)
    ]
    width = ordered_ref.shape[1]
    pieces = sems.shape[1]
    span = width // pieces
    bands = [slice(which * width, (which + 1) * width) for which in range(3)]
    blocks = [slice(piece * span, (piece + 1) * span) for piece in range(pieces)]
    copies = [
        [
            pltpu.make_async_copy(
                project_in_hbm.at[at, band], project_in_ref.at[at, band], sems.at[n, piece]
            )
            for piece, at in enumerate(blocks)
        ]
        for n, band in enumerate(bands)
    ]
    copies.append(
        [
            pltpu.make_async_copy(
                project_out_hbm.at[at, :], project_out_ref.at[at, :], sems.at[3, piece]
            )
            for piece, at in enumerate(blocks)
        ]
    )
    for copy in small_copies + sum(copies[:3], []):
        copy.start()
    for copy in small_copies:
        copy.wait()
    _, own_place = route_of(owner_ref, lax.axis_index("dp"), columns)

    lane = lax.broadcasted_iota(jnp.int32, (1, LANES), 1)
    lane_float = lane.astype(jnp.float32)
    image = segment_ref[...] % blk_count
    image_ref[...] = image
    image = image.astype(jnp.float32)
    image = jnp.transpose(jnp.broadcast_to(image, (LANES, tok_count)))
    image_is = image == lane_float
    for block in range(blk_count):
        at = slice(block * rows, (block + 1) * rows)
        blocked = jnp.zeros((1, LANES), jnp.float32)
        for other in range(blk_count):
            value = jnp.where(block_mask_ref[block, other] == 1, 0.0, NEGATIVE)
            blocked = jnp.where(lane == blk_count + other, value, blocked)
        query_mark_ref[at, :] = jnp.where(image_is[at], NEGATIVE, blocked).astype(jnp.bfloat16)
        block_is = jnp.where(lane == blk_count + block, 1.0, 0.0)
        key_mark_ref[at, :] = jnp.where(
            lane < blk_count, jnp.where(image_is[at], 0.0, 1.0), block_is
        ).astype(jnp.bfloat16)
    wide, experts = slot_keys_wide_ref.shape[0], slot_keys_ref.shape[0]
    column = lax.broadcasted_iota(jnp.int32, (wide, experts), 0)
    expert = lax.broadcasted_iota(jnp.int32, (wide, experts), 1)
    spread = jnp.where(column // blk_count == expert, 1.0, 0.0).astype(jnp.bfloat16)
    slot_keys_wide_ref[...] = dot(spread, slot_keys_ref[...]).astype(jnp.bfloat16)

    at = block_at(0 if certain else own_place, rows)
    block = own_ref[...]
    ordered_ref[at, :] = block
    normed = layer_norm(block.astype(jnp.float32)).astype(jnp.bfloat16)
    for n, band in enumerate(bands):
        for copy in copies[n]:
            copy.wait()
        if n == 0:
            for copy in copies[3]:
                copy.start()
        joint_ref[at, band] = dot(normed, project_in_ref[:, band]).astype(jnp.bfloat16)
    note_place(places_ref, 0, own_place)
    for copy in copies[3]:
        copy.wait()


def near_kernel(
    near_ref,
    project_in_ref,
    query_mark_ref,
    key_mark_ref,
    _ordered_ref,
    _joint_ref,
    _places_ref,
    ordered_ref,
    joint_ref,
    places_ref,
    *state,
    rows,
    certain,
):
    place = place_arrived(
        near_ref, 1 if certain else None, project_in_ref, ordered_ref, joint_ref
    )
    if not certain:
        return
    note_place(places_ref, 1, place)
    places = read_place(places_ref, 0), place
    attention = Attention(
        joint_ref,
        gathered(query_mark_ref, places, rows),
        gathered(key_mark_ref, places, rows),
    )
    span = slice(0, 2 * rows)
    tasks = []
    for pair in range(ordered_ref.shape[1] // LANES):
        kept = functools.partial(keep_state, state, pair, span)
        tasks.append(attention.begin(kept, pair, 0, 2 * rows, 2 * rows))
    staggered(tasks)


def middle_kernel(*refs, certain):
    *arrived, project_in_ref, query_mark_ref, key_mark_ref = refs[:-12]
    ordered_ref, joint_ref, places_ref, *state = refs[-6:]
    width = ordered_ref.shape[1]
    for slot, ref in enumerate(arrived, start=2):
        place = place_arrived(
            ref, slot if certain else None, project_in_ref, ordered_ref, joint_ref
        )
        if not certain:
            continue
        rows = ordered_ref.shape[0] // (len(arrived) + 3)
        note_place(places_ref, slot, place)
        places = [read_place(places_ref, n) for n in range(slot)] + [place]
        attention = Attention(
            joint_ref,
            gathered(query_mark_ref, places, rows),
            gathered(key_mark_ref, places, rows),
        )
        stop = slot * rows
        block = slice(stop, stop + rows)
        span = slice(0, stop)
        tasks = []
        for pair in range(width // LANES):
            kept, new = (functools.partial(keep_state, state, pair, at) for at in (span, block))
            old = functools.partial(read_state, state, pair, span)
            tasks.append(attention.extend(kept, pair, stop, block, old))
            tasks.append(attention.begin(new, pair, stop, stop + rows, stop + rows))
        staggered(tasks)


def front_kernel(
    arrived_ref,
    _ordered_ref,
    _joint_ref,
    places_ref,
    top_ref,
    picked_ref,
    total_ref,
    image_ref,
    query_mark_ref,
    key_mark_ref,
    project_in_ref,
    project_out_ref,
    slot_keys_ref,
    ordered_ref,
    joint_ref,
    hidden_ref,
    slot_in_ref,
    combine_ref,
    context_ref,
    moe_normed_ref,
    logits_ref,
    *,
    certain,
):
    tok_count, width = ordered_ref.shape
    blk_count = slot_in_ref.shape[1]
    rows = tok_count // blk_count
    last = blk_count - 1
    place = place_arrived(
        arrived_ref, last if certain else None, project_in_ref, ordered_ref, joint_ref
    )
    places = list(range(blk_count))
    if certain:
        places = [read_place(places_ref, n) for n in range(last)] + [place]
    attention = Attention(
        joint_ref,
        gathered(query_mark_ref, places, rows),
        gathered(key_mark_ref, places, rows),
    )
    state = top_ref, picked_ref, total_ref
    stop = last * rows if certain else 0

    def keep_context(pair, rows, tops, picked, total):
        at = slice(pair * LANES, (pair + 1) * LANES)
        context_ref[rows, at] = (picked / total).astype(jnp.bfloat16)

    column_image = lax.broadcasted_iota(jnp.int32, (logits_ref.shape[0], 1), 0) % blk_count

    def settle(slot, place):
        at, out = block_at(slot, rows), block_at(place, rows)
        projected = dot(context_ref[at, :], project_out_ref[...])
        yield
        hidden = (ordered_ref[at, :].astype(jnp.float32) + projected).astype(jnp.bfloat16)
        hidden_ref[out, :] = hidden
        moe_normed = layer_norm(hidden.astype(jnp.float32)).astype(jnp.bfloat16)
        moe_normed_ref[out, :] = moe_normed
        yield
        logits = dot(slot_keys_ref[...], moe_normed, ((1,), (1,)))
        logits_ref[:, out] = logits
        yield
        top = jnp.max(logits, axis=0, keepdims=True)
        member = image_ref[:, out] == column_image
        raised = jnp.where(member, jnp.exp(logits - top), 0.0)
        combine = raised / jnp.sum(raised, axis=0, keepdims=True)
        combine_ref[out, :] = jnp.transpose(combine.astype(jnp.bfloat16))

    span, block = slice(0, stop), slice(stop, tok_count)
    pairs = range(width // LANES)
    grown = [
        attention.extend(
            functools.partial(keep_context, pair, span),
            pair,
            stop,
            block,
            functools.partial(read_state, state, pair, span),
        )
        for pair in pairs
        if certain
    ]
    fresh = [
        attention.begin(functools.partial(keep_context, pair, block), pair, stop, tok_count, tok_count)
        for pair in pairs
    ]
    settled = [settle(slot, place) for slot, place in enumerate(places)]
    if certain:
        staggered(
            [*(task for both in zip(grown, fresh) for task in both), None, None, *settled]
        )
    else:
        staggered([*fresh, None, None, *settled])

    moe_normed = moe_normed_ref[...]
    logits = logits_ref[...]
    member = image_ref[...] == column_image
    top = jnp.max(jnp.where(member, logits, NEGATIVE), axis=1, keepdims=True)
    raised = jnp.where(member, jnp.exp(logits - top), 0.0)
    dispatch = raised / jnp.sum(raised, axis=1, keepdims=True)
    slot_in = dot(dispatch.astype(jnp.bfloat16), moe_normed)
    slot_in_ref[...] = slot_in.astype(jnp.bfloat16).reshape(slot_in_ref.shape)


def expert_kernel(arrived_ref, expert_in_ref, expert_out_ref, produced_ref, total_ref):
    rows, width = total_ref.shape
    slots = arrived_ref[...].reshape(rows, width)
    hidden_width = expert_in_ref.shape[2]
    step = math.gcd(hidden_width, 768)
    for at in range(0, hidden_width, step):
        inner = dot(slots, expert_in_ref[0, :, at : at + step])
        inner = 0.5 * inner * (1.0 + lax.erf(inner * math.sqrt(0.5)))
        part = dot(inner.astype(jnp.bfloat16), expert_out_ref[0, at : at + step, :])
        total_ref[...] = part if at == 0 else total_ref[...] + part
    produced_ref[...] = total_ref[...].astype(jnp.bfloat16).reshape(produced_ref.shape)


def combine_kernel(hidden_ref, combine_ref, returned_ref, out_hbm, out_ref, sems):
    returned = returned_ref[...].reshape(combine_ref.shape[1], hidden_ref.shape[1])
    count = sems.shape[0]
    rows = hidden_ref.shape[0] // count
    copies = []
    for n in range(count):
        at = slice(n * rows, (n + 1) * rows)
        mixture = dot(combine_ref[at, :], returned)
        out_ref[at, :] = (hidden_ref[at, :].astype(jnp.float32) + mixture).astype(jnp.bfloat16)
        copies.append(pltpu.make_async_copy(out_ref.at[at, :], out_hbm.at[at, :], sems.at[n]))
        copies[-1].start()
    for copy in copies:
        copy.wait()


def resident(*arrays, memory_space=pltpu.VMEM):
    return [pltpu.with_memory_space_constraint(array, memory_space) for array in arrays]


def whole(memory_space=pltpu.VMEM):
    return pl.BlockSpec(memory_space=memory_space)


def per_device(
    patches,
    owner_slot,
    segment_ids,
    block_mask,
    project_in,
    project_out,
    slot_keys,
    expert_in,
    expert_out,
):
    tok_count, width = patches.shape
    blk_count = owner_slot.shape[0]
    rows = tok_count // blk_count
    data_count = lax.axis_size("dp")
    column_count = lax.axis_size("expert")
    expert_count = slot_keys.shape[1]
    columns = expert_count * blk_count
    certain = data_count == blk_count
    params = pltpu.CompilerParams(vmem_limit_bytes=VMEM_LIMIT)

    flips = far_first(data_count)
    tiles = rows * width // (SUBLANES * LANES)
    *sends, own = pl.pallas_call(
        functools.partial(send_kernel, flips=flips, columns=column_count),
        out_shape=[pltpu.VMEM((tiles + 1, SUBLANES, LANES), jnp.bfloat16)] * len(flips)
        + [pltpu.VMEM((rows, width), jnp.bfloat16)],
        in_specs=[whole(pltpu.SMEM), whole()],
        out_specs=[whole()] * (len(flips) + 1),
        compiler_params=params,
        name="send",
    )(*resident(owner_slot, patches, memory_space=pltpu.HBM))
    arrived = []
    for flip, send in zip(flips, sends):
        arrived.append(lax.ppermute(send, "dp", [(i, i ^ flip) for i in range(data_count)]))
    far, near = arrived[:-1], arrived[-1]

    segment = segment_ids.reshape(1, tok_count)
    prepared = pl.pallas_call(
        functools.partial(prepare_kernel, columns=column_count, certain=certain),
        out_shape=[
            pltpu.VMEM(project_in.shape, jnp.bfloat16),
            pltpu.VMEM(project_out.shape, jnp.bfloat16),
            pltpu.VMEM((1, tok_count), jnp.int32),
            pltpu.VMEM((tok_count, LANES), jnp.bfloat16),
            pltpu.VMEM((tok_count, LANES), jnp.bfloat16),
            pltpu.VMEM((columns, width), jnp.bfloat16),
            pltpu.VMEM((tok_count, width), jnp.bfloat16),
            pltpu.VMEM((tok_count, 3 * width), jnp.bfloat16),
            pltpu.VMEM((data_count, LANES), jnp.float32),
        ],
        in_specs=[whole(pltpu.HBM)] * 4 + [whole()] + [whole(pltpu.HBM)] * 2,
        out_specs=[whole()] * 9,
        scratch_shapes=[
            pltpu.SMEM(owner_slot.shape, jnp.int32),
            pltpu.SMEM(block_mask.shape, jnp.int32),
            pltpu.VMEM(segment.shape, jnp.int32),
            pltpu.VMEM(slot_keys.shape[::-1], jnp.bfloat16),
            pltpu.SemaphoreType.DMA((4,)),
            pltpu.SemaphoreType.DMA((4, width // (2 * LANES))),
        ],
        compiler_params=params,
        name="prepare",
    )(
        *resident(owner_slot, block_mask, segment, slot_keys.T, memory_space=pltpu.HBM),
        *resident(own),
        *resident(project_in, project_out, memory_space=pltpu.HBM),
    )
    project_in, project_out, image, query_mark, key_mark, slot_keys_wide, *placed = prepared
    placed = pl.pallas_call(
        functools.partial(near_kernel, rows=rows, certain=certain),
        out_shape=[
            *(pltpu.VMEM(array.shape, array.dtype) for array in placed),
            pltpu.VMEM((width // HEAD, tok_count, LANES), jnp.float32),
            pltpu.VMEM((width // LANES, tok_count, LANES), jnp.float32),
            pltpu.VMEM((width // LANES, tok_count, LANES), jnp.float32),
        ],
        in_specs=[whole()] * 7,
        out_specs=[whole()] * 6,
        input_output_aliases={4 + n: n for n in range(3)},
        compiler_params=params,
        name="near",
    )(*resident(near, project_in, query_mark, key_mark, *placed))

    placed_shapes = tuple(pltpu.VMEM(array.shape, array.dtype) for array in placed)
    *earlier, last = far
    if earlier:
        base = len(earlier) + 3
        placed = pl.pallas_call(
            functools.partial(middle_kernel, certain=certain),
            out_shape=placed_shapes,
            in_specs=[whole()] * (base + len(placed)),
            out_specs=(whole(),) * len(placed),
            input_output_aliases={base + n: n for n in range(len(placed))},
            compiler_params=params,
            name="middle",
        )(*resident(*earlier, project_in, query_mark, key_mark, *placed))
    *_, hidden, slot_in, combine = pl.pallas_call(
        functools.partial(front_kernel, certain=certain),
        out_shape=(
            *placed_shapes[:2],
            pltpu.VMEM((tok_count, width), jnp.bfloat16),
            pltpu.VMEM((expert_count, blk_count, width), jnp.bfloat16),
            pltpu.VMEM((tok_count, columns), jnp.bfloat16),
        ),
        in_specs=[whole()] * 13,
        out_specs=(whole(),) * 5,
        input_output_aliases={1 + n: n for n in range(2)},
        scratch_shapes=[pltpu.VMEM((tok_count, width), jnp.bfloat16)] * 2
        + [pltpu.VMEM((columns, tok_count), jnp.float32)],
        compiler_params=params,
        name="front",
    )(
        *resident(last, *placed, image, query_mark, key_mark),
        *resident(project_in, project_out, slot_keys_wide),
    )
    slots_here = lax.all_to_all(slot_in, AXES, split_axis=0, concat_axis=0, tiled=True)
    produced = pl.pallas_call(
        expert_kernel,
        out_shape=pltpu.VMEM(slots_here.shape, jnp.bfloat16),
        in_specs=[whole()] * 3,
        out_specs=whole(),
        scratch_shapes=[pltpu.VMEM((columns, width), jnp.float32)],
        compiler_params=params,
        name="expert",
    )(*resident(slots_here, expert_in, expert_out))
    returned = lax.all_to_all(produced, AXES, split_axis=0, concat_axis=0, tiled=True)
    return pl.pallas_call(
        combine_kernel,
        out_shape=jax.ShapeDtypeStruct((tok_count, width), jnp.bfloat16),
        in_specs=[whole()] * 3,
        out_specs=whole(pltpu.HBM),
        scratch_shapes=[
            pltpu.VMEM((tok_count, width), jnp.bfloat16),
            pltpu.SemaphoreType.DMA((blk_count,)),
        ],
        compiler_params=params,
        name="combine",
    )(*resident(hidden, combine, returned))


def solution(mesh):
    in_specs = (
        P(AXES, None),
        P(AXES),
        P(AXES),
        P(AXES, None),
        P(),
        P(),
        P(),
        P(AXES, None, None),
        P(AXES, None, None),
    )
    return jax.shard_map(
        per_device,
        mesh=mesh,
        in_specs=in_specs,
        out_specs=P(AXES, None),
        check_vma=False,
    )
```
